256 devices in a mesh: gy: 64 (over x, y, z_hi, core), gz: 4 (over z_lo).
Axes of the slice: x: 4, y: 4, z: 8 (z_hi: 2, z_lo: 4; z = z_hi * 4 + z_lo), core: 2. Of those that a mesh axis runs over, the one named last changes fastest.
Arguments:
- efield_check: bfloat16 [3, 2048, 8, 1024], P(None, 'gy', None, 'gz'), may hold values from -6 to 6
- hfield_check: bfloat16 [3, 2048, 8, 1024], P(None, 'gy', None, 'gz'), may hold values from -6 to 6
- polar_check: bfloat16 [3, 2048, 8, 1024], P(None, 'gy', None, 'gz'), may hold values from -4 to 4
- rate_check: bfloat16 [3, 2048, 8, 1024], P(None, 'gy', None, 'gz'), may hold values from -4 to 4
- levels_check: bfloat16 [2, 2048, 8, 1024], P(None, 'gy', None, 'gz'), may hold values from 0.049804688 to 0.5
- efield_seed: float32 [3, 2048, 8, 1024], P(None, 'gy', None, 'gz'), may hold values from -6 to 6
- hfield_seed: float32 [3, 2048, 8, 1024], P(None, 'gy', None, 'gz'), may hold values from -6 to 6
- polar_seed: float32 [3, 2048, 8, 1024], P(None, 'gy', None, 'gz'), may hold values from -6 to 6
- rate_seed: float32 [3, 2048, 8, 1024], P(None, 'gy', None, 'gz'), may hold values from -6 to 6
- levels_seed: float32 [2, 2048, 8, 1024], P(None, 'gy', None, 'gz'), may hold values from -6 to 6
- material_labels: int32 [2048, 8, 1024], P('gy', None, 'gz'), may hold values from 0 to 3
- gain_labels: int32 [2048, 8, 1024], P('gy', None, 'gz'), may hold values 0 or 1
- inverse_table: float32 [4], replicated, may hold values from 0.08 to 1
- source_field: float32 [2048, 8, 1024], P('gy', None, 'gz'), may hold values from -6 to 6
- start_step: int32 [1], replicated, may hold values from 0 to 255
Outputs:
- efield_grad: float32 [3, 2048, 8, 1024], P(None, 'gy', None, 'gz')
- hfield_grad: float32 [3, 2048, 8, 1024], P(None, 'gy', None, 'gz')
- polar_grad: float32 [3, 2048, 8, 1024], P(None, 'gy', None, 'gz')
- rate_grad: float32 [3, 2048, 8, 1024], P(None, 'gy', None, 'gz')
- levels_grad: float32 [2, 2048, 8, 1024], P(None, 'gy', None, 'gz')
- cell_grad: float32 [2048, 8, 1024], P('gy', None, 'gz')
- table_grad: float32 [4], replicated
The draws below stay inside these ranges and needn't reach their ends.
All inputs are finite; a program needn't handle non-finite values. No bound on the sum of `gain_labels` on one device may be relied on, other than what follows from the above.
Results may differ from the reference program's by a relative error of at most 0.0003.
Values may be sent and summed in bfloat16 or wider, within the bound.
No kernel may reach another device: no remote copies, remote signals or barrier semaphores. Data moves between devices by JAX's collectives and lax.ppermute only.
A program may use at most 64 MiB of HBM per device.

```python
import math
import jax
import jax.numpy as jnp
from jax import lax

SLAB = 8
MATERIALS = 4
NY = 2048
NZ = 1024


def set_ends(values, rng, least, largest):
    longest = values.shape.index(max(values.shape))
    spots = []
    for shift in (0, 1):
        where = [jax.random.randint(jax.random.fold_in(rng, axis), (), 0, length) for axis, length in enumerate(values.shape)]
        where[longest] = (where[longest] + shift) % values.shape[longest]
        spots.append(tuple(where))
    return values.at[spots[0]].set(least).at[spots[1]].set(largest)


def level_of(own_key, dims, cuts, smallest, high):
    def one(dim, shards_of):
        heights = jax.random.uniform(jax.random.fold_in(jax.random.fold_in(own_key, 6), dim), (shards_of,), jnp.float32, smallest / len(cuts), high / len(cuts))
        return jnp.repeat(jnp.exp(heights), dims[dim] // shards_of).reshape((-1,) + (1,) * (len(dims) - dim - 1))

    factor_of = one(*cuts[0])
    for cut in cuts[1:]:
        factor_of = factor_of * one(*cut)
    return factor_of


def centred(stream_key, extent, scale, most, cuts=(), held_as=jnp.bfloat16):
    array = jax.random.normal(stream_key, extent, jnp.float32) * scale
    if len(cuts) > 0:
        array = level_of(stream_key, extent, cuts, -0.22, 0.18) * array
    return jnp.clip(array, min=-most, max=most).astype(held_as)


def setup_inputs(seed: int = 0) -> dict:
    keys = jax.random.split(jax.random.key(seed), 16)
    return {
        "efield_check": centred(keys[0], (3, NY, SLAB, NZ), 1.0, 6.0, ((1, 64), (3, 4))),
        "hfield_check": centred(keys[1], (3, NY, SLAB, NZ), 1.0, 6.0, ((1, 64), (3, 4))),
        "polar_check": centred(keys[2], (3, NY, SLAB, NZ), 0.5, 4.0, ((1, 64), (3, 4))),
        "rate_check": centred(keys[3], (3, NY, SLAB, NZ), 0.5, 4.0, ((1, 64), (3, 4))),
        "levels_check": jnp.clip(0.049804688 + 0.4501953 * jax.random.uniform(keys[4], (2, NY, SLAB, NZ), jnp.float32) ** level_of(keys[4], (2, NY, SLAB, NZ), ((1, 64), (3, 4)), -0.2, 0.2), 0.049804688, 0.5).astype(jnp.bfloat16),
        "efield_seed": centred(keys[5], (3, NY, SLAB, NZ), 1.0, 6.0, ((1, 64), (3, 4)), jnp.float32),
        "hfield_seed": centred(keys[6], (3, NY, SLAB, NZ), 1.0, 6.0, ((1, 64), (3, 4)), jnp.float32),
        "polar_seed": centred(keys[7], (3, NY, SLAB, NZ), 1.0, 6.0, ((1, 64), (3, 4)), jnp.float32),
        "rate_seed": centred(keys[8], (3, NY, SLAB, NZ), 1.0, 6.0, ((1, 64), (3, 4)), jnp.float32),
        "levels_seed": centred(keys[9], (2, NY, SLAB, NZ), 1.0, 6.0, ((1, 64), (3, 4)), jnp.float32),
        "material_labels": set_ends(jax.random.randint(keys[10], (NY, SLAB, NZ), 0, MATERIALS), jax.random.fold_in(keys[10], 1), 0, MATERIALS - 1).astype(jnp.int32),
        "gain_labels": set_ends((jax.random.randint(keys[11], (NY, SLAB, NZ), 0, 2) < 1).astype(jnp.int32), jax.random.fold_in(keys[11], 1), 0, 1),
        "inverse_table": jnp.clip(jnp.exp(jax.random.uniform(keys[12], (MATERIALS,), jnp.float32, math.log(0.08), math.log(1.0))), 0.08, 1.0),
        "source_field": centred(keys[13], (NY, SLAB, NZ), 1.0, 6.0, ((0, 64), (2, 4)), jnp.float32),
        "start_step": jax.random.randint(keys[14], (1,), 0, 256).astype(jnp.int32),
    }


MAGNETIC_STEP = 0.5
ELECTRIC_STEP = 0.5
TIME_STEP = 0.5
DAMPING = 0.9
STIFFNESS = 0.3
COUPLING = 0.4
PUMPING = 0.05
UPPER_DECAY = 0.02
LOWER_DECAY = 0.3
STIMULATED = 0.2
SOURCE_OMEGA = 0.35

def front(values, axis):
    rest = lax.slice_in_dim(values, 1, values.shape[axis], axis=axis)
    border = jnp.zeros_like(lax.slice_in_dim(values, 0, 1, axis=axis))
    return jnp.concatenate([rest, border], axis)

def behind(values, axis):
    rest = lax.slice_in_dim(values, 0, values.shape[axis] - 1, axis=axis)
    border = jnp.zeros_like(lax.slice_in_dim(values, 0, 1, axis=axis))
    return jnp.concatenate([border, rest], axis)

def curl_from(along_x, along_y, along_z):
    return jnp.stack([along_y[2] - along_z[1], along_z[0] - along_x[2], along_x[1] - along_y[0]])

def curl_forward(field):
    return curl_from(front(field, 2) - field, front(field, 1) - field, front(field, 3) - field)

def curl_backward(field):
    return curl_from(field - behind(field, 2), field - behind(field, 1), field - behind(field, 3))

def local_update(efield, polar_field, polar_rate, levels, curl_field, inverse, gain_region, source_push):
    rate_next = DAMPING * polar_rate - STIFFNESS * polar_field + COUPLING * gain_region * (levels[0] - levels[1]) * efield
    polar_next = polar_field + TIME_STEP * rate_next
    forcing = ELECTRIC_STEP * curl_field - (polar_next - polar_field)
    forcing = jnp.concatenate([forcing[:2], forcing[2:] - source_push[None]], 0)
    efield_next = efield + inverse * forcing
    stimulated = STIMULATED * gain_region * lax.optimization_barrier(jnp.sum(efield_next * rate_next, axis=0))
    upper = levels[0] + TIME_STEP * (PUMPING * (1.0 - levels[0] - levels[1]) - UPPER_DECAY * levels[0]) - stimulated
    lower = levels[1] + TIME_STEP * (UPPER_DECAY * levels[0] - LOWER_DECAY * levels[1]) + stimulated
    return (efield_next, polar_next, rate_next, jnp.stack([upper, lower]))

def reverse_local(efield, polar_field, polar_rate, levels, curl_field, inverse, gain_region, source_push, seeds):

    def update(first, second, third, fourth, fifth, sixth):
        return local_update(first, second, third, fourth, fifth, sixth, gain_region, source_push)
    unused, pullback = jax.vjp(update, efield, polar_field, polar_rate, levels, curl_field, inverse)
    return pullback(seeds)

def material_map(material_labels, inverse_table):
    inverse = jnp.zeros(material_labels.shape, jnp.float32)
    for label in range(inverse_table.shape[0]):
        inverse = inverse + jnp.where(material_labels == label, inverse_table[label], jnp.float32(0.0))
    return inverse

def label_sums(material_labels, values, count):
    return jnp.stack([jnp.sum(jnp.where(material_labels == label, values, jnp.float32(0.0))) for label in range(count)])

def reference(efield_check, hfield_check, polar_check, rate_check, levels_check, efield_seed, hfield_seed, polar_seed, rate_seed, levels_seed, material_labels, gain_labels, inverse_table, source_field, start_step):
    inverse = material_map(material_labels, inverse_table)
    gain_region = gain_labels.astype(jnp.float32)
    start = start_step[0].astype(jnp.float32)
    push_first = jnp.sin(SOURCE_OMEGA * start) * source_field
    push_second = jnp.sin(SOURCE_OMEGA * (start + 1.0)) * source_field
    efield = efield_check.astype(jnp.float32)
    hfield = hfield_check.astype(jnp.float32)
    polar_field = polar_check.astype(jnp.float32)
    polar_rate = rate_check.astype(jnp.float32)
    levels = levels_check.astype(jnp.float32)
    hfield_mid = hfield - MAGNETIC_STEP * curl_forward(efield)
    curl_first = curl_backward(hfield_mid)
    state_one = local_update(efield, polar_field, polar_rate, levels, curl_first, inverse, gain_region, push_first)
    hfield_next = hfield_mid - MAGNETIC_STEP * curl_forward(state_one[0])
    curl_second = curl_backward(hfield_next)
    back_e, back_p, back_q, back_n, back_c, grad_second = reverse_local(state_one[0], state_one[1], state_one[2], state_one[3], curl_second, inverse, gain_region, push_second, (efield_seed, polar_seed, rate_seed, levels_seed))
    h_back = hfield_seed + curl_forward(back_c)
    e_back = back_e - MAGNETIC_STEP * curl_backward(h_back)
    last_e, polar_grad, rate_grad, levels_grad, last_c, grad_first = reverse_local(efield, polar_field, polar_rate, levels, curl_first, inverse, gain_region, push_first, (e_back, back_p, back_q, back_n))
    hfield_grad = h_back + curl_forward(last_c)
    efield_grad = last_e - MAGNETIC_STEP * curl_backward(hfield_grad)
    cell_grad = grad_second + grad_first
    table_grad = label_sums(material_labels, cell_grad, inverse_table.shape[0]) * (1.0 / math.sqrt(NY * SLAB * NZ))
    return (efield_grad, hfield_grad, polar_grad, rate_grad, levels_grad, cell_grad, table_grad)
```

```python
import math

import jax
import jax.numpy as jnp
from jax import lax
from jax.sharding import PartitionSpec as P

MAGNETIC_STEP = 0.5
ELECTRIC_STEP = 0.5
TIME_STEP = 0.5
DAMPING = 0.9
STIFFNESS = 0.3
COUPLING = 0.4
PUMPING = 0.05
UPPER_DECAY = 0.02
LOWER_DECAY = 0.3
STIMULATED = 0.2
SOURCE_OMEGA = 0.35


def shifted(block, axis, distance):
    devices = range(lax.axis_size(axis))
    route = [(i - distance, i) for i in devices if i - distance in devices]
    inner = [pair for pair in route if min(pair) % 2 == 0]
    outer = [pair for pair in route if min(pair) % 2 == 1]
    far = lax.ppermute(block, axis, outer)
    near = lax.ppermute(block, axis, inner)
    return far + near


def shifted_column(column, distance):
    shape = column.shape
    moved = shifted(column.reshape(shape[0], -1), "gz", distance)
    return moved.reshape(shape)


def front(values, axis):
    rest = lax.slice_in_dim(values, 1, values.shape[axis], axis=axis)
    border = jnp.zeros_like(lax.slice_in_dim(values, 0, 1, axis=axis))
    return jnp.concatenate([rest, border], axis)


def behind(values, axis):
    rest = lax.slice_in_dim(values, 0, values.shape[axis] - 1, axis=axis)
    border = jnp.zeros_like(lax.slice_in_dim(values, 0, 1, axis=axis))
    return jnp.concatenate([border, rest], axis)


def curl_from(along_x, along_y, along_z):
    return jnp.stack([along_y[2] - along_z[1], along_z[0] - along_x[2], along_x[1] - along_y[0]])


def curl_forward(field):
    front_row = shifted(field[:, :1], "gy", -1)
    front_column = shifted_column(field[:, :, :, :1], -1)
    along_y = jnp.concatenate([field[:, 1:], front_row], 1) - field
    along_z = jnp.concatenate([field[:, :, :, 1:], front_column], 3) - field
    along_x = front(field, 2) - field
    return curl_from(along_x, along_y, along_z)


def curl_backward(field):
    back_row = shifted(field[:, -1:], "gy", 1)
    back_column = shifted_column(field[:, :, :, -1:], 1)
    along_y = field - jnp.concatenate([back_row, field[:, :-1]], 1)
    along_z = field - jnp.concatenate([back_column, field[:, :, :, :-1]], 3)
    along_x = field - behind(field, 2)
    return curl_from(along_x, along_y, along_z)


def local_update(
    efield, polar_field, polar_rate, levels, curl_field, inverse, gain_region, source_push
):
    rate_next = (
        DAMPING * polar_rate
        - STIFFNESS * polar_field
        + COUPLING * gain_region * (levels[0] - levels[1]) * efield
    )
    polar_next = polar_field + TIME_STEP * rate_next
    forcing = ELECTRIC_STEP * curl_field - (polar_next - polar_field)
    forcing = jnp.concatenate([forcing[:2], forcing[2:] - source_push[None]], 0)
    efield_next = efield + inverse * forcing
    stimulated = STIMULATED * gain_region * jnp.sum(efield_next * rate_next, axis=0)
    upper = (
        levels[0]
        + TIME_STEP * (PUMPING * (1.0 - levels[0] - levels[1]) - UPPER_DECAY * levels[0])
        - stimulated
    )
    lower = levels[1] + TIME_STEP * (UPPER_DECAY * levels[0] - LOWER_DECAY * levels[1]) + stimulated
    return (efield_next, polar_next, rate_next, jnp.stack([upper, lower]))


def reverse_local(
    efield, polar_field, polar_rate, levels, curl_field, inverse, gain_region, source_push, seeds
):

    def update(first, second, third, fourth, fifth, sixth):
        return local_update(first, second, third, fourth, fifth, sixth, gain_region, source_push)

    unused, pullback = jax.vjp(update, efield, polar_field, polar_rate, levels, curl_field, inverse)
    return pullback(seeds)


def material_map(material_labels, inverse_table):
    inverse = jnp.zeros(material_labels.shape, jnp.float32)
    for label in range(inverse_table.shape[0]):
        inverse = inverse + jnp.where(
            material_labels == label, inverse_table[label], jnp.float32(0.0)
        )
    return inverse


def label_sums(material_labels, values, count):
    return jnp.stack(
        [
            jnp.sum(jnp.where(material_labels == label, values, jnp.float32(0.0)))
            for label in range(count)
        ]
    )


def everywhere_sum(values):
    axes = ("gy", "gz")
    devices = lax.axis_size("gy") * lax.axis_size("gz")
    sent = jnp.broadcast_to(values[None, None], (devices, 1, values.shape[0]))
    return jnp.sum(lax.all_to_all(sent, axes, 0, 0), axis=(0, 1))


def on_device(
    efield_check,
    hfield_check,
    polar_check,
    rate_check,
    levels_check,
    efield_seed,
    hfield_seed,
    polar_seed,
    rate_seed,
    levels_seed,
    material_labels,
    gain_labels,
    inverse_table,
    source_field,
    start_step,
):
    count = inverse_table.shape[0]
    inverse = material_map(material_labels, inverse_table)
    gain_region = gain_labels.astype(jnp.float32)
    start = start_step[0].astype(jnp.float32)
    first_sine = jnp.sin(SOURCE_OMEGA * start)
    push_first = first_sine * source_field
    push_second = jnp.sin(SOURCE_OMEGA * (start + 1.0)) * source_field
    efield = efield_check.astype(jnp.float32)
    polar_field = polar_check.astype(jnp.float32)
    polar_rate = rate_check.astype(jnp.float32)
    levels = levels_check.astype(jnp.float32)
    hfield = hfield_check.astype(jnp.float32)
    hfield_mid = hfield - MAGNETIC_STEP * curl_forward(efield)
    curl_first = curl_backward(hfield_mid)
    state_one = local_update(
        efield, polar_field, polar_rate, levels, curl_first, inverse, gain_region, push_first
    )
    hfield_next = hfield_mid - MAGNETIC_STEP * curl_forward(state_one[0])
    curl_second = curl_backward(hfield_next)
    back_e, back_p, back_q, back_n, back_c, grad_second = reverse_local(
        state_one[0],
        state_one[1],
        state_one[2],
        state_one[3],
        curl_second,
        inverse,
        gain_region,
        push_second,
        (efield_seed, polar_seed, rate_seed, levels_seed),
    )
    h_back = hfield_seed + curl_forward(back_c)
    e_back = back_e - MAGNETIC_STEP * curl_backward(h_back)
    last_e, polar_grad, rate_grad, levels_grad, last_c, grad_first = reverse_local(
        efield,
        polar_field,
        polar_rate,
        levels,
        curl_first,
        inverse,
        gain_region,
        push_first,
        (e_back, back_p, back_q, back_n),
    )
    hfield_grad = h_back + curl_forward(last_c)
    efield_grad = last_e - MAGNETIC_STEP * curl_backward(hfield_grad)
    cell_grad = grad_second + grad_first
    cells = (
        material_labels.shape[0]
        * material_labels.shape[1]
        * material_labels.shape[2]
        * lax.axis_size("gy")
        * lax.axis_size("gz")
    )
    totals = everywhere_sum(label_sums(material_labels, cell_grad, count))
    table_grad = totals * (1.0 / math.sqrt(cells))
    return (efield_grad, hfield_grad, polar_grad, rate_grad, levels_grad, cell_grad, table_grad)


def solution(mesh):
    placed = (
        P(None, "gy", None, "gz"),
        P(None, "gy", None, "gz"),
        P(None, "gy", None, "gz"),
        P(None, "gy", None, "gz"),
        P(None, "gy", None, "gz"),
        P(None, "gy", None, "gz"),
        P(None, "gy", None, "gz"),
        P(None, "gy", None, "gz"),
        P(None, "gy", None, "gz"),
        P(None, "gy", None, "gz"),
        P("gy", None, "gz"),
        P("gy", None, "gz"),
        P(),
        P("gy", None, "gz"),
        P(),
    )
    return jax.shard_map(
        on_device,
        mesh=mesh,
        in_specs=placed,
        out_specs=(
            P(None, "gy", None, "gz"),
            P(None, "gy", None, "gz"),
            P(None, "gy", None, "gz"),
            P(None, "gy", None, "gz"),
            P(None, "gy", None, "gz"),
            P("gy", None, "gz"),
            P(),
        ),
        check_vma=False,
    )
```

```python
import math

import jax
import jax.numpy as jnp
import numpy as np
from jax import lax
from jax.experimental import pallas as pl
from jax.experimental.pallas import tpu as pltpu
from jax.sharding import PartitionSpec as P

SOURCE_OMEGA = 0.35
F32 = jnp.float32
BF16 = jnp.bfloat16
NAMES = ("E", "H", "P", "Q", "N", "lab", "gain", "src", "Es", "Ns", "Hs", "Ps", "Qs")
COUNT = dict(E=3, H=3, P=3, Q=3, N=2, lab=1, gain=1, src=1, Es=3, Ns=2, Hs=3, Ps=3, Qs=3)
WIDTH = dict(E=3, H=3, P=2, Q=2, N=2, lab=2, gain=2, src=2, Es=2, Ns=2, Hs=2, Ps=1, Qs=1)
HALF = ("E", "H", "P", "Q", "N")
COMPS = [(name, c) for name in NAMES for c in range(COUNT[name])]
INDEX = {comp: i for i, comp in enumerate(COMPS)}
SPOT, PLANE, IS_FRONT = {}, {}, np.zeros((1, 128), np.int32)
_lane, _plane = 0, 0
for _comp in COMPS:
    _w = WIDTH[_comp[0]]
    SPOT[_comp] = _lane + _w
    IS_FRONT[0, _lane + _w : _lane + 2 * _w] = 1
    PLANE[_comp] = _plane
    _lane += 2 * _w
    _plane += _w
PLANES = _plane
LANES = 384
EDGE = 9


def lane_of(shape):
    return lax.broadcasted_iota(jnp.int32, shape, 1)


def pull(ref, comp, index):
    name, c = comp
    if COUNT[name] == 1:
        value = ref[index].astype(F32)
        return value + 1.0 if name == "lab" else value
    return ref[c, index].astype(F32)


def take(ref, comp, start, count):
    if COUNT[comp[0]] == 1:
        return ref.at[pl.ds(start, count)]
    return ref.at[comp[1], pl.ds(start, count)]


def pack_rows(rows, *refs):
    given = dict(zip(NAMES, refs[: len(NAMES)]))
    messages = refs[len(NAMES) : len(NAMES) + 2]
    floats, ints, sems = refs[len(NAMES) + 2 :]
    even = lax.rem(lax.axis_index("gy"), 2) == 0
    started, later = [], []
    for side in range(2):
        last = even if side == 0 else jnp.logical_not(even)
        wide = ints_at = 0
        for comp in COMPS:
            w = WIDTH[comp[0]]
            start = jnp.where(last, rows - w, 0)
            source = take(given[comp[0]], comp, start, w)
            if comp[0] in HALF:
                target = messages[side].at[pl.ds(PLANE[comp], w)]
            elif comp[0] in ("lab", "gain"):
                target = ints.at[side, pl.ds(ints_at, w)]
                later.append((side, comp, ints, ints_at))
                ints_at += w
            else:
                target = floats.at[side, pl.ds(wide, w)]
                later.append((side, comp, floats, wide))
                wide += w
            copy = pltpu.make_async_copy(source, target, sems.at[side, INDEX[comp]])
            copy.start()
            started.append(copy)
    for copy in started:
        copy.wait()
    for side, comp, held, at in later:
        for k in range(WIDTH[comp[0]]):
            value = held[side, at + k].astype(F32)
            if comp[0] == "lab":
                value = value + 1.0
            messages[side][PLANE[comp] + k] = value.astype(BF16)


def pack_columns(*refs):
    given = dict(zip(NAMES, refs[: len(NAMES)]))
    first, second = refs[len(NAMES) :]
    even = lax.rem(lax.axis_index("gz"), 2) == 0
    lane = lane_of((8, 128))

    def row(y, carry):
        low = jnp.zeros((8, 128), F32)
        high = jnp.zeros((8, 128), F32)
        for comp in reversed(COMPS):
            value = pull(given[comp[0]], comp, y)
            inside = lane < SPOT[comp] + WIDTH[comp[0]]
            low = jnp.where(inside, pltpu.roll(value[:, :128], SPOT[comp], 1), low)
            high = jnp.where(inside, pltpu.roll(value[:, 128:], SPOT[comp], 1), high)
        first[y] = jnp.where(even, high, low).astype(BF16)
        second[y] = jnp.where(even, low, high).astype(BF16)
        return carry

    lax.fori_loop(0, first.shape[0], row, 0)


def curl_ahead(v, above):
    inside = lax.broadcasted_iota(jnp.int32, v[0].shape, 0) < 7
    size = v[0].shape[1]

    def dz(c):
        return pltpu.roll(v[c], size - 1, 1) - v[c]

    def dx(c):
        return jnp.where(inside, pltpu.roll(v[c], 7, 0), 0.0) - v[c]

    return [
        (above[2] - v[2]) - dz(1),
        dz(0) - dx(2),
        dx(1) - (above[0] - v[0]),
    ]


def curl_back(v, below):
    inside = lax.broadcasted_iota(jnp.int32, v[0].shape, 0) > 0

    def dz(c):
        return v[c] - pltpu.roll(v[c], 1, 1)

    def dx(c):
        return v[c] - jnp.where(inside, pltpu.roll(v[c], 1, 0), 0.0)

    return [
        (v[2] - below[2]) - dz(1),
        dz(0) - dx(2),
        dx(1) - (v[0] - below[0]),
    ]


SCRATCH = dict(M=3, E1=3, Q1=3, F1=3, Q2=3, aE=3, aC=3, bH=3, cC=3, cE=3, hg=3, inv=1, g2=1, k0=1, k1=1)


def six_stages(get, put, held, bases, count, table, push_first, push_second, keep_row, keep_lane):
    def load(name, row):
        return [held[name][c, row] for c in range(SCRATCH[name])]

    def store(name, row, values):
        for c, value in enumerate(values):
            held[name][c, row] = value

    def kept(values, row):
        return [value * (keep_lane * keep_row(row)) for value in values]

    def trio(name, row):
        return [get((name, c), row) for c in range(3)]

    def over(low, high, body):
        if len(bases) == 1:
            lax.fori_loop(low, high, lambda r, carry: (body(r), carry)[1], 0)
        else:
            span = high - low
            step = bases[1] - bases[0]

            def walk(i, carry):
                chunk = i // span
                body(chunk * step + (i - chunk * span) + low + bases[0])
                return carry

            lax.fori_loop(0, span * len(bases), walk, 0)

    def stage_one(r):
        above = {0: get(("E", 0), r + 1), 2: get(("E", 2), r + 1)}
        curl = curl_ahead(trio("E", r), above)
        store("M", r, kept([h - 0.5 * c for h, c in zip(trio("H", r), curl)], r))

    def stage_two(r):
        electric, polar, rate = trio("E", r), trio("P", r), trio("Q", r)
        upper, lower = get(("N", 0), r), get(("N", 1), r)
        label, gain, source = get(("lab", 0), r), get(("gain", 0), r), get(("src", 0), r)
        inverse = jnp.zeros_like(label)
        for m, value in enumerate(table):
            inverse = jnp.where(label == m + 1.0, value, inverse)
        g2, g4 = 0.2 * gain, 0.4 * gain
        k0 = g4 * (upper - lower)
        q1 = [0.9 * q - 0.3 * p + k0 * e for q, p, e in zip(rate, polar, electric)]
        p1 = [p + 0.5 * q for p, q in zip(polar, q1)]
        curl = curl_back(load("M", r), {0: held["M"][0, r - 1], 2: held["M"][2, r - 1]})
        f1 = [0.5 * (c - q) for c, q in zip(curl, q1)]
        f1[2] = f1[2] - push_first * source
        e1 = [e + inverse * f for e, f in zip(electric, f1)]
        s1 = g2 * sum(e * q for e, q in zip(e1, q1))
        up = upper + 0.5 * (0.05 * (1.0 - upper - lower) - 0.02 * upper)
        low = lower + 0.5 * (0.02 * upper - 0.3 * lower)
        k1 = g4 * (up - low - 2.0 * s1)
        q2 = [0.9 * q - 0.3 * p + k1 * e for q, p, e in zip(q1, p1, e1)]
        sb = g2 * (get(("Ns", 1), r) - get(("Ns", 0), r))
        a_e = [e + sb * q for e, q in zip(trio("Es", r), q2)]
        half = 0.5 * inverse
        store("E1", r, e1)
        store("Q1", r, q1)
        store("F1", r, f1)
        store("Q2", r, q2)
        store("aE", r, a_e)
        store("aC", r, [half * a for a in a_e])
        store("inv", r, [inverse])
        store("g2", r, [g2])
        store("k0", r, [k0])
        store("k1", r, [k1])

    def stage_three(r):
        e1 = curl_ahead(load("E1", r), {0: held["E1"][0, r + 1], 2: held["E1"][2, r + 1]})
        store("M", r, kept([m - 0.5 * c for m, c in zip(load("M", r), e1)], r))
        a_c = curl_ahead(load("aC", r), {0: held["aC"][0, r + 1], 2: held["aC"][2, r + 1]})
        store("bH", r, kept([h + c for h, c in zip(trio("Hs", r), a_c)], r))

    def stage_four(r):
        (inverse,), (g2,), (k0,), (k1,) = load("inv", r), load("g2", r), load("k0", r), load("k1", r)
        up, low = get(("Ns", 0), r), get(("Ns", 1), r)
        sb = g2 * (low - up)
        curl = curl_back(load("M", r), {0: held["M"][0, r - 1], 2: held["M"][2, r - 1]})
        q2, e1, a_e = load("Q2", r), load("E1", r), load("aE", r)
        f2 = [0.5 * (c - q) for c, q in zip(curl, q2)]
        f2[2] = f2[2] - push_second * get(("src", 0), r)
        e2 = [e + inverse * f for e, f in zip(e1, f2)]
        grad = sum(a * f for a, f in zip(a_e, f2))
        p_seed = trio("Ps", r)
        qt = [
            q + sb * e + 0.5 * (p - inverse * a)
            for q, e, p, a in zip(trio("Qs", r), e2, p_seed, a_e)
        ]
        a_p = [p - 0.3 * q for p, q in zip(p_seed, qt)]
        dn = 2.0 * g2 * sum(q * e for q, e in zip(qt, e1))
        a_up = 0.965 * up + 0.01 * low + dn
        a_low = 0.85 * low - 0.025 * up - dn
        curl = curl_back(load("bH", r), {0: held["bH"][0, r - 1], 2: held["bH"][2, r - 1]})
        sb = g2 * (a_low - a_up)
        q1 = load("Q1", r)
        c_e = [
            a + k1 * q - 0.5 * c + sb * p for a, q, c, p in zip(a_e, qt, curl, q1)
        ]
        half = 0.5 * inverse
        store("cC", r, [half * c for c in c_e])
        grad = grad + sum(c * f for c, f in zip(c_e, load("F1", r)))

        def own(value):
            return value[:, :256]

        inverse, g2, k0, sb = own(inverse), own(g2), own(k0), own(sb)
        q_out, e_out = [], []
        dn = 0.0
        for c in range(3):
            pt = own(a_p[c]) - inverse * own(c_e[c])
            q = 0.9 * own(qt[c]) + sb * own(e1[c]) + 0.5 * pt
            q_out.append(q)
            dn = dn + q * own(get(("E", c), r))
            held["cE"][c, r] = own(c_e[c]) + k0 * q
        dn = 2.0 * g2 * dn
        a_up, a_low = own(a_up), own(a_low)
        put("polar", r, [own(p) - 0.3 * q for p, q in zip(a_p, q_out)])
        put("rate", r, [0.9 * q for q in q_out])
        put("levels", r, [0.965 * a_up + 0.01 * a_low + dn, 0.85 * a_low - 0.025 * a_up - dn])
        put("cell", r, [own(grad)])

    def stage_five(r):
        curl = curl_ahead(load("cC", r), {0: held["cC"][0, r + 1], 2: held["cC"][2, r + 1]})
        hg = kept([h + c for h, c in zip(load("bH", r), curl)], r)
        store("hg", r, hg)

    def stage_six(r):
        hg = load("hg", r)
        curl = curl_back(hg, {0: held["hg"][0, r - 1], 2: held["hg"][2, r - 1]})
        put("h", r, [h[:, :256] for h in hg])
        put("e", r, [held["cE"][c, r] - 0.5 * curl[c][:, :256] for c in range(3)])

    over(0, count - 1, stage_one)
    over(1, count - 1, stage_two)
    over(1, count - 2, stage_three)
    over(2, count - 2, stage_four)
    over(2, count - 3, stage_five)
    over(3, count - 3, stage_six)


OUTS = ("e", "h", "polar", "rate", "levels", "cell")
OUT_COMPS = dict(e=3, h=3, polar=3, rate=3, levels=2, cell=1)
HELD = tuple(SCRATCH)


def lane_keep():
    lane = lane_of((1, LANES))
    outside = jnp.logical_and(lax.axis_index("gz") == 0, lane >= 320)
    return jnp.where(outside, 0.0, 1.0).astype(F32)


def material_sums(totals, label, value):
    for m in range(totals.shape[0]):
        totals[m] = totals[m] + jnp.where(label == m + 1.0, value, 0.0)


def inner_kernel(rows, *refs):
    n = len(NAMES)
    given = dict(zip(NAMES, refs[:n]))
    tiles, table_ref, push_ref = refs[n : n + 3]
    outs = dict(zip(OUTS, refs[n + 3 : n + 3 + len(OUTS)]))
    totals = refs[n + 3 + len(OUTS)]
    held = dict(zip(HELD, refs[n + 4 + len(OUTS) :]))
    totals[...] = jnp.zeros_like(totals)

    def get(comp, r):
        third = pltpu.roll(tiles[r], 128 - SPOT[comp], 1)
        return jnp.concatenate([pull(given[comp[0]], comp, r), third], 1)

    def put(name, r, values):
        if OUT_COMPS[name] == 1:
            outs[name][r] = values[0]
        else:
            for c, value in enumerate(values):
                outs[name][c, r] = value

    table = [table_ref[m] for m in range(table_ref.shape[0])]
    six_stages(
        get, put, held, (0,), rows, table, push_ref[0], push_ref[1], lambda r: 1.0, lane_keep()
    )

    def add(r, carry):
        material_sums(totals, given["lab"][r].astype(F32) + 1.0, outs["cell"][r])
        return carry

    lax.fori_loop(3, rows - 3, add, 0)


def edge_kernel(rows, *refs):
    n = len(NAMES)
    given = dict(zip(NAMES, refs[:n]))
    tiles, near, far, near_tiles, far_tiles, table_ref, push_ref, inner_totals = refs[n : n + 8]
    at = n + 8 + len(OUTS)
    outs = dict(zip(OUTS, refs[at : at + len(OUTS)]))
    totals = refs[at + len(OUTS)]
    at += len(OUTS) + 1
    ext = refs[at]
    staged = dict(zip(OUTS, refs[at + 1 : at + 1 + len(OUTS)]))
    at += 1 + len(OUTS)
    held = dict(zip(HELD, refs[at : at + len(HELD)]))
    sems = refs[at + len(HELD)]
    even = lax.rem(lax.axis_index("gy"), 2) == 0
    top = lax.axis_index("gy") == 0

    for side in range(2):
        for comp in COMPS:
            w = WIDTH[comp[0]]
            for r in range(EDGE):
                own = r - 3 if side == 0 else rows - 6 + r
                if 0 <= own < rows:
                    main = pull(given[comp[0]], comp, own)
                    tile = tiles[own]
                else:
                    k = r - (3 - w) if side == 0 else r - 6
                    if not 0 <= k < w:
                        continue
                    at_plane = PLANE[comp] + k
                    main_near = near[at_plane].astype(F32)
                    main_far = far[at_plane].astype(F32)
                    t = r if side == 0 else r - 6
                    tile_near, tile_far = near_tiles[t].astype(F32), far_tiles[t].astype(F32)
                    use_far = even if side == 0 else jnp.logical_not(even)
                    main = jnp.where(use_far, main_far, main_near)
                    tile = jnp.where(use_far, tile_far, tile_near)
                third = pltpu.roll(tile, 128 - SPOT[comp], 1)
                ext[INDEX[comp], side * EDGE + r] = jnp.concatenate([main, third], 1)

    def get(comp, r):
        return ext[INDEX[comp], r]

    def put(name, r, values):
        for c, value in enumerate(values):
            staged[name][c, r] = value

    def keep_row(r):
        return jnp.where(jnp.logical_and(top, r < 3), 0.0, 1.0).astype(F32)

    table = [table_ref[m] for m in range(table_ref.shape[0])]
    six_stages(
        get, put, held, (0, EDGE), EDGE, table, push_ref[0], push_ref[1], keep_row, lane_keep()
    )
    copies = []
    for side in range(2):
        for i, name in enumerate(OUTS):
            source = staged[name].at[:, pl.ds(side * EDGE + 3, 3)]
            start = 0 if side == 0 else rows - 3
            if OUT_COMPS[name] == 1:
                source = staged[name].at[0, pl.ds(side * EDGE + 3, 3)]
                target = outs[name].at[pl.ds(start, 3)]
            else:
                target = outs[name].at[:, pl.ds(start, 3)]
            copy = pltpu.make_async_copy(source, target, sems.at[side, i])
            copy.start()
            copies.append(copy)
    totals[...] = inner_totals[...]
    for side in range(2):
        for k in range(3):
            r = side * EDGE + 3 + k
            material_sums(totals, ext[INDEX[("lab", 0)], r, :, :256], staged["cell"][0, r])
    for copy in copies:
        copy.wait()


def swapped(block, axes, reach, odd):
    size = [lax.axis_size(a) for a in ("gy", "gz")]
    pairs = []
    for y in range(size[0]):
        for z in range(size[1]):
            y2, z2 = (y + 1, z) if axes == "gy" else (y, z + 1)
            at = y if axes == "gy" else z
            if at % 2 == odd and y2 < size[0] and z2 < size[1]:
                one, two = y * size[1] + z, y2 * size[1] + z2
                pairs += [(one, two), (two, one)]
    return lax.ppermute(block, ("gy", "gz"), pairs)


def on_device(
    efield_check,
    hfield_check,
    polar_check,
    rate_check,
    levels_check,
    efield_seed,
    hfield_seed,
    polar_seed,
    rate_seed,
    levels_seed,
    material_labels,
    gain_labels,
    inverse_table,
    source_field,
    start_step,
):
    given = (
        efield_check,
        hfield_check,
        polar_check,
        rate_check,
        levels_check,
        material_labels,
        gain_labels,
        source_field,
        efield_seed,
        levels_seed,
        hfield_seed,
        polar_seed,
        rate_seed,
    )
    rows = material_labels.shape[0]
    count = inverse_table.shape[0]
    start = start_step[0].astype(F32)
    pushes = jnp.stack([jnp.sin(SOURCE_OMEGA * start), jnp.sin(SOURCE_OMEGA * (start + 1.0))])
    anywhere = pl.BlockSpec(memory_space=pl.ANY)
    vmem = pl.BlockSpec(memory_space=pltpu.VMEM)
    smem = pl.BlockSpec(memory_space=pltpu.SMEM)
    message = jax.ShapeDtypeStruct((PLANES, 8, 256), BF16)
    limit = pltpu.CompilerParams(vmem_limit_bytes=60 * 1024 * 1024)

    send_near, send_far = pl.pallas_call(
        lambda *refs: pack_rows(rows, *refs),
        out_shape=(message, message),
        in_specs=[anywhere] * len(given),
        out_specs=(vmem, vmem),
        scratch_shapes=[
            pltpu.VMEM((2, 26, 8, 256), F32),
            pltpu.VMEM((2, 4, 8, 256), jnp.int32),
            pltpu.SemaphoreType.DMA((2, len(COMPS))),
        ],
        name="pack_rows",
    )(*given)
    far = swapped(send_far, "gy", 1, 1)
    near = swapped(send_near, "gy", 1, 0)

    tile_shape = jax.ShapeDtypeStruct((rows, 8, 128), BF16)
    send_first, send_second = pl.pallas_call(
        pack_columns,
        out_shape=(tile_shape, tile_shape),
        in_specs=[vmem] * len(given),
        out_specs=(vmem, vmem),
        compiler_params=limit,
        name="pack_columns",
    )(*given)
    first = swapped(send_first, "gz", 1, 0)
    second = swapped(send_second, "gz", 1, 1)
    even_z = lax.rem(lax.axis_index("gz"), 2) == 0
    even_y = lax.rem(lax.axis_index("gy"), 2) == 0
    tiles = jnp.where((IS_FRONT[None] == 1) == even_z, first, second)
    last, begin = tiles[rows - 3 :], tiles[:3]
    far_tiles = swapped(jnp.where(even_y, begin, last), "gy", 1, 1)
    near_tiles = swapped(jnp.where(even_y, last, begin), "gy", 1, 0)
    tiles = tiles.astype(F32)

    def out_shape(name):
        dims = (rows, 8, 256)
        return jax.ShapeDtypeStruct(dims if OUT_COMPS[name] == 1 else (OUT_COMPS[name],) + dims, F32)

    def held(size):
        return [
            pltpu.VMEM((SCRATCH[name], size, 8, 256 if name == "cE" else LANES), F32)
            for name in HELD
        ]

    sums = jax.ShapeDtypeStruct((count, 8, 256), F32)
    *inner, totals = pl.pallas_call(
        lambda *refs: inner_kernel(rows, *refs),
        out_shape=tuple(out_shape(name) for name in OUTS) + (sums,),
        in_specs=[vmem] * (len(given) + 1) + [smem, smem],
        out_specs=(vmem,) * (len(OUTS) + 1),
        scratch_shapes=held(rows),
        compiler_params=limit,
        cost_estimate=pl.CostEstimate(flops=40_000_000, bytes_accessed=12_000_000, transcendentals=0),
        name="inner_rows",
    )(*given, tiles, inverse_table, pushes)

    n = len(given) + 8
    *outs, totals = pl.pallas_call(
        lambda *refs: edge_kernel(rows, *refs),
        out_shape=tuple(out_shape(name) for name in OUTS) + (sums,),
        in_specs=[vmem] * (len(given) + 5) + [smem, smem, vmem] + [anywhere] * len(OUTS),
        out_specs=(anywhere,) * len(OUTS) + (vmem,),
        scratch_shapes=[pltpu.VMEM((len(COMPS), 2 * EDGE, 8, LANES), F32)]
        + [pltpu.VMEM((OUT_COMPS[name], 2 * EDGE, 8, 256), F32) for name in OUTS]
        + held(2 * EDGE)
        + [pltpu.SemaphoreType.DMA((2, len(OUTS)))],
        input_output_aliases={n + i: i for i in range(len(OUTS))},
        compiler_params=limit,
        cost_estimate=pl.CostEstimate(flops=16_000_000, bytes_accessed=6_000_000, transcendentals=0),
        name="edge_rows",
    )(*given, tiles, near, far, near_tiles, far_tiles, inverse_table, pushes, totals, *inner)

    devices = lax.axis_size("gy") * lax.axis_size("gz")
    cells = rows * material_labels.shape[1] * material_labels.shape[2] * devices
    part = jnp.sum(totals, axis=(1, 2))
    sent = jnp.broadcast_to(part[None, None], (devices, 1, count))
    table_grad = jnp.sum(lax.all_to_all(sent, ("gy", "gz"), 0, 0), axis=(0, 1)) * (
        1.0 / math.sqrt(cells)
    )
    return (*outs, table_grad)


def solution(mesh):
    field = P(None, "gy", None, "gz")
    cell = P("gy", None, "gz")
    return jax.shard_map(
        on_device,
        mesh=mesh,
        in_specs=(field,) * 10 + (cell, cell, P(), cell, P()),
        out_specs=(field,) * 5 + (cell, P()),
        check_vma=False,
    )
```

```python
import math

import jax
import jax.numpy as jnp
import numpy as np
from jax import lax
from jax.experimental import pallas as pl
from jax.experimental.pallas import tpu as pltpu
from jax.sharding import PartitionSpec as P

SOURCE_OMEGA = 0.35
F32 = jnp.float32
BF16 = jnp.bfloat16
NAMES = ("E", "H", "P", "Q", "N", "lab", "gain", "src", "Es", "Ns", "Hs", "Ps", "Qs")
COUNT = dict(E=3, H=3, P=3, Q=3, N=2, lab=1, gain=1, src=1, Es=3, Ns=2, Hs=3, Ps=3, Qs=3)
WIDTH = dict(E=3, H=3, P=2, Q=2, N=2, lab=2, gain=2, src=2, Es=2, Ns=2, Hs=2, Ps=1, Qs=1)
HALF = ("E", "H", "P", "Q", "N")
COMPS = [(name, c) for name in NAMES for c in range(COUNT[name])]
INDEX = {comp: i for i, comp in enumerate(COMPS)}
SPOT, PLANE, IS_FRONT = {}, {}, np.zeros((1, 128), np.int32)
_lane, _plane = 0, 0
for _comp in COMPS:
    _w = WIDTH[_comp[0]]
    SPOT[_comp] = _lane + _w
    IS_FRONT[0, _lane + _w : _lane + 2 * _w] = 1
    PLANE[_comp] = _plane
    _lane += 2 * _w
    _plane += _w
LOW_BITS = _plane
CORNERS = LOW_BITS + 3
PLANES = CORNERS + 2
LANES = 384
EDGE = 9


def lane_of(shape):
    return lax.broadcasted_iota(jnp.int32, shape, 1)


def pull(ref, comp, index):
    name, c = comp
    if COUNT[name] == 1:
        value = ref[index].astype(F32)
        return value + 1.0 if name == "lab" else value
    return ref[c, index].astype(F32)


def take(ref, comp, start, count):
    if COUNT[comp[0]] == 1:
        return ref.at[pl.ds(start, count)]
    return ref.at[comp[1], pl.ds(start, count)]


def pack_rows(rows, *refs):
    given = dict(zip(NAMES, refs[: len(NAMES)]))
    messages = refs[len(NAMES) : len(NAMES) + 2]
    floats, ints, sems = refs[len(NAMES) + 2 :]
    even = lax.rem(lax.axis_index("gy"), 2) == 0
    started, later = [], []
    for side in range(2):
        last = even if side == 0 else jnp.logical_not(even)
        wide = ints_at = 0
        for comp in COMPS:
            w = WIDTH[comp[0]]
            start = jnp.where(last, rows - w, 0)
            source = take(given[comp[0]], comp, start, w)
            if comp[0] in HALF:
                target = messages[side].at[pl.ds(PLANE[comp], w)]
            elif comp[0] in ("lab", "gain"):
                target = ints.at[side, pl.ds(ints_at, w)]
                later.append((side, comp, ints, ints_at))
                ints_at += w
            else:
                target = floats.at[side, pl.ds(wide, w)]
                later.append((side, comp, floats, wide))
                wide += w
            copy = pltpu.make_async_copy(source, target, sems.at[side, INDEX[comp]])
            copy.start()
            started.append(copy)
    for copy in started:
        copy.wait()
    for side, comp, held, at in later:
        for k in range(WIDTH[comp[0]]):
            value = held[side, at + k].astype(F32)
            if comp[0] == "lab":
                value = value + 1.0
            messages[side][PLANE[comp] + k] = value.astype(BF16)
        if comp[0] == "Hs":
            last = even if side == 0 else jnp.logical_not(even)
            value = jnp.where(last, held[side, at + 1], held[side, at])
            low = value - value.astype(BF16).astype(F32)
            messages[side][LOW_BITS + comp[1]] = low.astype(BF16)


def pack_columns(*refs):
    given = dict(zip(NAMES, refs[: len(NAMES)]))
    first, second = refs[len(NAMES) :]
    even = lax.rem(lax.axis_index("gz"), 2) == 0
    lane = lane_of((8, 128))

    def some(block, carry):
        ys = [block * 4 + k for k in range(4)]
        low = [jnp.zeros((8, 128), F32) for y in ys]
        high = [jnp.zeros((8, 128), F32) for y in ys]
        for comp in reversed(COMPS):
            inside = lane < SPOT[comp] + WIDTH[comp[0]]
            for k, y in enumerate(ys):
                value = pull(given[comp[0]], comp, y)
                low[k] = jnp.where(inside, pltpu.roll(value[:, :128], SPOT[comp], 1), low[k])
                high[k] = jnp.where(inside, pltpu.roll(value[:, 128:], SPOT[comp], 1), high[k])
        for k, y in enumerate(ys):
            first[y] = jnp.where(even, high[k], low[k]).astype(BF16)
            second[y] = jnp.where(even, low[k], high[k]).astype(BF16)
        return carry

    lax.fori_loop(0, first.shape[0] // 4, some, 0)


def curl_ahead(v, above):
    inside = lax.broadcasted_iota(jnp.int32, v[0].shape, 0) < 7
    size = v[0].shape[1]

    def dz(c):
        return pltpu.roll(v[c], size - 1, 1) - v[c]

    def dx(c):
        return jnp.where(inside, pltpu.roll(v[c], 7, 0), 0.0) - v[c]

    return [
        (above[2] - v[2]) - dz(1),
        dz(0) - dx(2),
        dx(1) - (above[0] - v[0]),
    ]


def curl_back(v, below):
    inside = lax.broadcasted_iota(jnp.int32, v[0].shape, 0) > 0

    def dz(c):
        return v[c] - pltpu.roll(v[c], 1, 1)

    def dx(c):
        return v[c] - jnp.where(inside, pltpu.roll(v[c], 1, 0), 0.0)

    return [
        (v[2] - below[2]) - dz(1),
        dz(0) - dx(2),
        dx(1) - (v[0] - below[0]),
    ]


SCRATCH = dict(
    M=3, W=3, E1=3, Q1=3, F1=3, Q2=3, aE=3, aC=3, bH=3, cC=3, cE=3, hg=3, inv=1, g2=1, k0=1, k1=1
)


def six_stages(
    get, put, tally, held, bases, count, table, push_first, push_second, keep_row, keep_lane, flushes
):
    def load(name, row):
        return [held[name][c, row] for c in range(SCRATCH[name])]

    def pair(name, row):
        return {0: held[name][0, row], 2: held[name][2, row]}

    def store(name, row, values):
        for c, value in enumerate(values):
            held[name][c, row] = value

    def kept(values, row):
        done = []
        for value in values:
            value = jnp.concatenate([value[:, :256], value[:, 256:] * keep_lane], 1)
            done.append(value if keep_row is None else value * keep_row(row))
        return done

    def trio(name, row):
        return [get((name, c), row) for c in range(3)]

    def stage_one(r):
        above = {0: get(("E", 0), r + 1), 2: get(("E", 2), r + 1)}
        curl = curl_ahead(trio("E", r), above)
        store("M", r, kept([h - 0.5 * c for h, c in zip(trio("H", r), curl)], r))

    def stage_two(r):
        electric, polar, rate = trio("E", r), trio("P", r), trio("Q", r)
        upper, lower = get(("N", 0), r), get(("N", 1), r)
        label, gain, source = get(("lab", 0), r), get(("gain", 0), r), get(("src", 0), r)
        inverse = jnp.zeros_like(label)
        for m, value in enumerate(table):
            inverse = jnp.where(label == m + 1.0, value, inverse)
        g2, g4 = 0.2 * gain, 0.4 * gain
        k0 = g4 * (upper - lower)
        q1 = [0.9 * q - 0.3 * p + k0 * e for q, p, e in zip(rate, polar, electric)]
        p1 = [p + 0.5 * q for p, q in zip(polar, q1)]
        curl = curl_back(load("M", r), pair("M", r - 1))
        f1 = [0.5 * (c - q) for c, q in zip(curl, q1)]
        f1[2] = f1[2] - push_first * source
        e1 = [e + inverse * f for e, f in zip(electric, f1)]
        s1 = g2 * sum(e * q for e, q in zip(e1, q1))
        up = upper + 0.5 * (0.05 * (1.0 - upper - lower) - 0.02 * upper)
        low = lower + 0.5 * (0.02 * upper - 0.3 * lower)
        k1 = g4 * (up - low - 2.0 * s1)
        q2 = [0.9 * q - 0.3 * p + k1 * e for q, p, e in zip(q1, p1, e1)]
        sb = g2 * (get(("Ns", 1), r) - get(("Ns", 0), r))
        a_e = [e + sb * q for e, q in zip(trio("Es", r), q2)]
        half = 0.5 * inverse
        store("E1", r, e1)
        store("Q1", r, q1)
        store("F1", r, f1)
        store("Q2", r, q2)
        store("aE", r, a_e)
        store("aC", r, [half * a for a in a_e])
        store("inv", r, [inverse])
        store("g2", r, [g2])
        store("k0", r, [k0])
        store("k1", r, [k1])

    def stage_three(r):
        curl = curl_ahead(load("E1", r), pair("E1", r + 1))
        store("W", r, kept([m - 0.5 * c for m, c in zip(load("M", r), curl)], r))
        curl = curl_ahead(load("aC", r), pair("aC", r + 1))
        store("bH", r, kept([h + c for h, c in zip(trio("Hs", r), curl)], r))

    def stage_four(r):
        (inverse,), (g2,), (k0,), (k1,) = load("inv", r), load("g2", r), load("k0", r), load("k1", r)
        up, low = get(("Ns", 0), r), get(("Ns", 1), r)
        sb = g2 * (low - up)
        curl = curl_back(load("W", r), pair("W", r - 1))
        q2, e1, a_e = load("Q2", r), load("E1", r), load("aE", r)
        f2 = [0.5 * (c - q) for c, q in zip(curl, q2)]
        f2[2] = f2[2] - push_second * get(("src", 0), r)
        e2 = [e + inverse * f for e, f in zip(e1, f2)]
        grad = sum(a[:, :256] * f[:, :256] for a, f in zip(a_e, f2))
        p_seed = trio("Ps", r)
        qt = [
            q + sb * e + 0.5 * (p - inverse * a)
            for q, e, p, a in zip(trio("Qs", r), e2, p_seed, a_e)
        ]
        dn = 2.0 * g2 * sum(q * e for q, e in zip(qt, e1))
        a_up = 0.965 * up + 0.01 * low + dn
        a_low = 0.85 * low - 0.025 * up - dn
        curl = curl_back(load("bH", r), pair("bH", r - 1))
        sb = g2 * (a_low - a_up)
        c_e = [
            a + k1 * q - 0.5 * c + sb * p for a, q, c, p in zip(a_e, qt, curl, load("Q1", r))
        ]
        half = 0.5 * inverse
        store("cC", r, [half * c for c in c_e])

        def own(value):
            return value[:, :256]

        grad = grad + sum(own(c) * own(f) for c, f in zip(c_e, load("F1", r)))
        inverse, g2, k0, sb = own(inverse), own(g2), own(k0), own(sb)
        p_out, q_out = [], []
        dn = 0.0
        for c in range(3):
            a_p = own(p_seed[c]) - 0.3 * own(qt[c])
            pt = a_p - inverse * own(c_e[c])
            q = 0.9 * own(qt[c]) + sb * own(e1[c]) + 0.5 * pt
            p_out.append(a_p - 0.3 * q)
            q_out.append(0.9 * q)
            dn = dn + q * own(get(("E", c), r))
            held["cE"][c, r] = own(c_e[c]) + k0 * q
        dn = 2.0 * g2 * dn
        a_up, a_low = own(a_up), own(a_low)
        put("polar", r, p_out)
        put("rate", r, q_out)
        put("levels", r, [0.965 * a_up + 0.01 * a_low + dn, 0.85 * a_low - 0.025 * a_up - dn])
        put("cell", r, [grad])

    def stage_five(r):
        curl = curl_ahead(load("cC", r), pair("cC", r + 1))
        store("hg", r, kept([h + c for h, c in zip(load("bH", r), curl)], r))

    def stage_six(r):
        hg = load("hg", r)
        curl = curl_back(hg, pair("hg", r - 1))
        put("h", r, [h[:, :256] for h in hg])
        put("e", r, [held["cE"][c, r] - 0.5 * curl[c][:, :256] for c in range(3)])
        tally(r)

    plan = (
        (stage_six, 7, 3, count - 3),
        (stage_five, 6, 2, count - 3),
        (stage_four, 4, 2, count - 2),
        (stage_three, 3, 1, count - 2),
        (stage_two, 1, 1, count - 1),
        (stage_one, 0, 0, count - 1),
    )
    marks = {low + lag for _, lag, low, high in plan} | {high + lag for _, lag, low, high in plan}
    marks = sorted(marks | {row + 7 for row in flushes})
    for begin, end in zip(marks, marks[1:]):
        active = [(f, lag) for f, lag, low, high in plan if low + lag <= begin and end <= high + lag]

        def body(i, carry, active=active):
            for f, lag in active:
                for base in bases:
                    f(i - lag + base)
            return carry

        if end - begin == 1:
            body(begin, 0)
        else:
            lax.fori_loop(begin, end, body, 0)
        if end - 7 in flushes:
            flushes[end - 7]()


OUTS = ("e", "h", "polar", "rate", "levels", "cell")
OUT_COMPS = dict(e=3, h=3, polar=3, rate=3, levels=2, cell=1)
HELD = tuple(SCRATCH)


def lane_keep():
    lane = lane_of((1, 128))
    outside = jnp.logical_and(lax.axis_index("gz") == 0, lane >= 64)
    return jnp.where(outside, 0.0, 1.0).astype(F32)


def material_sums(totals, label, value):
    for m in range(totals.shape[0]):
        totals[m] = totals[m] + jnp.where(label == m + 1.0, value, 0.0)


def inner_kernel(rows, *refs):
    n = len(NAMES)
    given = dict(zip(NAMES, refs[:n]))
    tiles, table_ref, push_ref = refs[n : n + 3]
    at = n + 3
    outs = dict(zip(OUTS, refs[at : at + len(OUTS)]))
    totals = refs[at + len(OUTS)]
    at += len(OUTS) + 1
    staged = dict(zip(OUTS, refs[at : at + len(OUTS)]))
    at += len(OUTS)
    held = dict(zip(HELD, refs[at : at + len(HELD)]))
    sems = refs[at + len(HELD)]
    totals[...] = jnp.zeros_like(totals)

    def get(comp, r):
        third = pltpu.roll(tiles[r], 128 - SPOT[comp], 1)
        return jnp.concatenate([pull(given[comp[0]], comp, r), third], 1)

    def put(name, r, values):
        for c, value in enumerate(values):
            staged[name][c, r] = value

    def tally(r):
        material_sums(totals, given["lab"][r].astype(F32) + 1.0, staged["cell"][0, r])

    copies = []

    def leave(piece, low, high):
        for i, name in enumerate(OUTS):
            if OUT_COMPS[name] == 1:
                source = staged[name].at[0, pl.ds(low, high - low)]
                target = outs[name].at[pl.ds(low, high - low)]
            else:
                source = staged[name].at[:, pl.ds(low, high - low)]
                target = outs[name].at[:, pl.ds(low, high - low)]
            copy = pltpu.make_async_copy(source, target, sems.at[piece, i])
            copy.start()
            copies.append(copy)

    cuts = [3, 14, 22, rows - 3]
    flushes = {
        high: (lambda piece=piece, low=low, high=high: leave(piece, low, high))
        for piece, (low, high) in enumerate(zip(cuts, cuts[1:]))
    }
    table = [table_ref[m] for m in range(table_ref.shape[0])]
    six_stages(
        get,
        put,
        tally,
        held,
        (0,),
        rows,
        table,
        push_ref[0],
        push_ref[1],
        None,
        lane_keep(),
        flushes,
    )
    for copy in copies:
        copy.wait()


def edge_kernel(rows, *refs):
    n = len(NAMES)
    given = dict(zip(NAMES, refs[:n]))
    tiles, near, far, table_ref, push_ref, inner_totals = refs[n : n + 6]
    at = n + 6 + len(OUTS)
    outs = dict(zip(OUTS, refs[at : at + len(OUTS)]))
    totals = refs[at + len(OUTS)]
    at += len(OUTS) + 1
    ext = refs[at]
    staged = dict(zip(OUTS, refs[at + 1 : at + 1 + len(OUTS)]))
    at += 1 + len(OUTS)
    held = dict(zip(HELD, refs[at : at + len(HELD)]))
    sems = refs[at + len(HELD)]
    even = lax.rem(lax.axis_index("gy"), 2) == 0
    top = lax.axis_index("gy") == 0

    def arrived(use_far, plane):
        return jnp.where(use_far, far[plane].astype(F32), near[plane].astype(F32))

    for side in range(2):
        for comp in COMPS:
            w = WIDTH[comp[0]]
            for r in range(EDGE):
                own = r - 3 if side == 0 else rows - 6 + r
                if 0 <= own < rows:
                    main = pull(given[comp[0]], comp, own)
                    tile = tiles[own]
                else:
                    k = r - (3 - w) if side == 0 else r - 6
                    if not 0 <= k < w:
                        continue
                    use_far = even if side == 0 else jnp.logical_not(even)
                    main = arrived(use_far, PLANE[comp] + k)
                    if comp[0] == "Hs" and r == (2 if side == 0 else 6):
                        main = main + arrived(use_far, LOW_BITS + comp[1])
                    t = r if side == 0 else r - 6
                    tile = arrived(use_far, CORNERS + t // 2)
                    tile = tile[:, (t % 2) * 128 : (t % 2) * 128 + 128]
                third = pltpu.roll(tile, 128 - SPOT[comp], 1)
                ext[INDEX[comp], side * EDGE + r] = jnp.concatenate([main, third], 1)

    def get(comp, r):
        return ext[INDEX[comp], r]

    def put(name, r, values):
        for c, value in enumerate(values):
            staged[name][c, r] = value

    def keep_row(r):
        return jnp.where(jnp.logical_and(top, r < 3), 0.0, 1.0).astype(F32)

    totals[...] = inner_totals[...]

    def tally(r):
        material_sums(totals, ext[INDEX[("lab", 0)], r, :, :256], staged["cell"][0, r])

    table = [table_ref[m] for m in range(table_ref.shape[0])]
    six_stages(
        get,
        put,
        tally,
        held,
        (0, EDGE),
        EDGE,
        table,
        push_ref[0],
        push_ref[1],
        keep_row,
        lane_keep(),
        {},
    )
    copies = []
    for side in range(2):
        for i, name in enumerate(OUTS):
            source = staged[name].at[:, pl.ds(side * EDGE + 3, 3)]
            start = 0 if side == 0 else rows - 3
            if OUT_COMPS[name] == 1:
                source = staged[name].at[0, pl.ds(side * EDGE + 3, 3)]
                target = outs[name].at[pl.ds(start, 3)]
            else:
                target = outs[name].at[:, pl.ds(start, 3)]
            copy = pltpu.make_async_copy(source, target, sems.at[side, i])
            copy.start()
            copies.append(copy)
    for copy in copies:
        copy.wait()


def swapped(block, axes, odd):
    size = [lax.axis_size(a) for a in ("gy", "gz")]
    pairs = []
    for y in range(size[0]):
        for z in range(size[1]):
            y2, z2 = (y + 1, z) if axes == "gy" else (y, z + 1)
            at = y if axes == "gy" else z
            if at % 2 == odd and y2 < size[0] and z2 < size[1]:
                one, two = y * size[1] + z, y2 * size[1] + z2
                pairs += [(one, two), (two, one)]
    return lax.ppermute(block, ("gy", "gz"), pairs)


def on_device(
    efield_check,
    hfield_check,
    polar_check,
    rate_check,
    levels_check,
    efield_seed,
    hfield_seed,
    polar_seed,
    rate_seed,
    levels_seed,
    material_labels,
    gain_labels,
    inverse_table,
    source_field,
    start_step,
):
    given = (
        efield_check,
        hfield_check,
        polar_check,
        rate_check,
        levels_check,
        material_labels,
        gain_labels,
        source_field,
        efield_seed,
        levels_seed,
        hfield_seed,
        polar_seed,
        rate_seed,
    )
    rows = material_labels.shape[0]
    count = inverse_table.shape[0]
    start = start_step[0].astype(F32)
    pushes = jnp.stack([jnp.sin(SOURCE_OMEGA * start), jnp.sin(SOURCE_OMEGA * (start + 1.0))])
    anywhere = pl.BlockSpec(memory_space=pl.ANY)
    vmem = pl.BlockSpec(memory_space=pltpu.VMEM)
    smem = pl.BlockSpec(memory_space=pltpu.SMEM)
    message = jax.ShapeDtypeStruct((PLANES, 8, 256), BF16)
    limit = pltpu.CompilerParams(vmem_limit_bytes=30 * 1024 * 1024)

    tile_shape = jax.ShapeDtypeStruct((rows, 8, 128), BF16)
    blocks = 4

    def row_block(array):
        if array.ndim == 3:
            return pl.BlockSpec((rows // blocks, 8, 256), lambda i: (i, 0, 0))
        return pl.BlockSpec((array.shape[0], rows // blocks, 8, 256), lambda i: (0, i, 0, 0))

    tile_block = pl.BlockSpec((rows // blocks, 8, 128), lambda i: (i, 0, 0))
    send_first, send_second = pl.pallas_call(
        pack_columns,
        grid=(blocks,),
        out_shape=(tile_shape, tile_shape),
        in_specs=[row_block(array) for array in given],
        out_specs=(tile_block, tile_block),
        compiler_params=pltpu.CompilerParams(vmem_limit_bytes=6 * 1024 * 1024),
        name="pack_columns",
    )(*given)
    first = swapped(send_first, "gz", 0)
    second = swapped(send_second, "gz", 1)
    send_near, send_far = pl.pallas_call(
        lambda *refs: pack_rows(rows, *refs),
        out_shape=(message, message),
        in_specs=[anywhere] * len(given),
        out_specs=(vmem, vmem),
        scratch_shapes=[
            pltpu.VMEM((2, 24, 8, 256), F32),
            pltpu.VMEM((2, 4, 8, 256), jnp.int32),
            pltpu.SemaphoreType.DMA((2, len(COMPS))),
        ],
        compiler_params=pltpu.CompilerParams(vmem_limit_bytes=6 * 1024 * 1024),
        name="pack_rows",
    )(*given)
    even_z = lax.rem(lax.axis_index("gz"), 2) == 0
    even_y = lax.rem(lax.axis_index("gy"), 2) == 0
    tiles = jnp.where((IS_FRONT[None] == 1) == even_z, first, second)

    def corners(of):
        upper = jnp.concatenate([of[0], of[1]], 1)
        return jnp.stack([upper, jnp.concatenate([of[2], of[2]], 1)])

    last, begin = corners(tiles[rows - 3 :]), corners(tiles[:3])
    send_far = send_far.at[CORNERS:].set(jnp.where(even_y, begin, last))
    send_near = send_near.at[CORNERS:].set(jnp.where(even_y, last, begin))
    far = swapped(send_far, "gy", 1)
    near = swapped(send_near, "gy", 0)
    tiles = tiles.astype(F32)

    def out_shape(name):
        dims = (rows, 8, 256)
        return jax.ShapeDtypeStruct(dims if OUT_COMPS[name] == 1 else (OUT_COMPS[name],) + dims, F32)

    def held(size):
        return [
            pltpu.VMEM((SCRATCH[name], size, 8, 256 if name == "cE" else LANES), F32)
            for name in HELD
        ]

    sums = jax.ShapeDtypeStruct((count, 8, 256), F32)
    *inner, totals = pl.pallas_call(
        lambda *refs: inner_kernel(rows, *refs),
        out_shape=tuple(out_shape(name) for name in OUTS) + (sums,),
        in_specs=[vmem] * (len(given) + 1) + [smem, smem],
        out_specs=(anywhere,) * len(OUTS) + (vmem,),
        scratch_shapes=[pltpu.VMEM((OUT_COMPS[name], rows, 8, 256), F32) for name in OUTS]
        + held(rows)
        + [pltpu.SemaphoreType.DMA((3, len(OUTS)))],
        compiler_params=limit,
        cost_estimate=pl.CostEstimate(flops=40_000_000, bytes_accessed=12_000_000, transcendentals=0),
        name="inner_rows",
    )(*given, tiles, inverse_table, pushes)

    n = len(given) + 6
    *outs, totals = pl.pallas_call(
        lambda *refs: edge_kernel(rows, *refs),
        out_shape=tuple(out_shape(name) for name in OUTS) + (sums,),
        in_specs=[vmem] * (len(given) + 3) + [smem, smem, vmem] + [anywhere] * len(OUTS),
        out_specs=(anywhere,) * len(OUTS) + (vmem,),
        scratch_shapes=[pltpu.VMEM((len(COMPS), 2 * EDGE, 8, LANES), F32)]
        + [pltpu.VMEM((OUT_COMPS[name], 2 * EDGE, 8, 256), F32) for name in OUTS]
        + held(2 * EDGE)
        + [pltpu.SemaphoreType.DMA((2, len(OUTS)))],
        input_output_aliases={n + i: i for i in range(len(OUTS))},
        compiler_params=limit,
        cost_estimate=pl.CostEstimate(flops=16_000_000, bytes_accessed=6_000_000, transcendentals=0),
        name="edge_rows",
    )(*given, tiles, near, far, inverse_table, pushes, totals, *inner)

    devices = lax.axis_size("gy") * lax.axis_size("gz")
    cells = rows * material_labels.shape[1] * material_labels.shape[2] * devices
    part = jnp.sum(totals, axis=(1, 2))
    sent = jnp.broadcast_to(part[None, None], (devices, 1, count))
    table_grad = jnp.sum(lax.all_to_all(sent, ("gy", "gz"), 0, 0), axis=(0, 1)) * (
        1.0 / math.sqrt(cells)
    )
    return (*outs, table_grad)


def solution(mesh):
    field = P(None, "gy", None, "gz")
    cell = P("gy", None, "gz")
    return jax.shard_map(
        on_device,
        mesh=mesh,
        in_specs=(field,) * 10 + (cell, cell, P(), cell, P()),
        out_specs=(field,) * 5 + (cell, P()),
        check_vma=False,
    )
```

```python
import math

import jax
import jax.numpy as jnp
import numpy as np
from jax import lax
from jax.experimental import pallas as pl
from jax.experimental.pallas import tpu as pltpu
from jax.sharding import PartitionSpec as P

SOURCE_OMEGA = 0.35
F32 = jnp.float32
BF16 = jnp.bfloat16
NAMES = ("E", "H", "P", "Q", "N", "lab", "gain", "src", "Es", "Ns", "Hs", "Ps", "Qs")
COUNT = dict(E=3, H=3, P=3, Q=3, N=2, lab=1, gain=1, src=1, Es=3, Ns=2, Hs=3, Ps=3, Qs=3)
WIDTH = dict(E=3, H=3, P=2, Q=2, N=2, lab=2, gain=2, src=2, Es=2, Ns=2, Hs=2, Ps=1, Qs=1)
HALF = ("E", "H", "P", "Q", "N")
COMPS = [(name, c) for name in NAMES for c in range(COUNT[name])]
INDEX = {comp: i for i, comp in enumerate(COMPS)}
SPOT, PLANE, IS_FRONT = {}, {}, np.zeros((1, 128), np.int32)
_lane, _plane = 0, 0
for _comp in COMPS:
    _w = WIDTH[_comp[0]]
    SPOT[_comp] = _lane + _w
    IS_FRONT[0, _lane + _w : _lane + 2 * _w] = 1
    PLANE[_comp] = _plane
    _lane += 2 * _w
    _plane += _w
LOW_BITS = _plane
CORNERS = LOW_BITS + 3
PLANES = CORNERS + 2
LANES = 384
EDGE = 9


def lane_of(shape):
    return lax.broadcasted_iota(jnp.int32, shape, 1)


def pull(ref, comp, index):
    name, c = comp
    if COUNT[name] == 1:
        value = ref[index].astype(F32)
        return value + 1.0 if name == "lab" else value
    return ref[c, index].astype(F32)


def take(ref, comp, start, count):
    if COUNT[comp[0]] == 1:
        return ref.at[pl.ds(start, count)]
    return ref.at[comp[1], pl.ds(start, count)]


def go(copies):
    for copy in copies:
        copy.start()
    return copies


def wait(copies):
    for copy in copies:
        copy.wait()


def pack_rows(rows, *refs):
    n = len(NAMES)
    given = dict(zip(NAMES, refs[:n]))
    tile_inputs, front_ref = refs[n : n + 2], refs[n + 2]
    tile_out, outs = refs[n + 3], refs[n + 4 : n + 6]
    messages, floats, ints, tile_in, tiles, sems, other_sems = refs[n + 6 :]
    even = lax.rem(lax.axis_index("gy"), 2) == 0
    even_z = lax.rem(lax.axis_index("gz"), 2) == 0
    tile_copies = go(
        [pltpu.make_async_copy(tile_inputs[i], tile_in.at[i], other_sems.at[i]) for i in range(2)]
    )
    started, later = [], []
    for side in range(2):
        last = even if side == 0 else jnp.logical_not(even)
        wide = ints_at = 0
        for comp in COMPS:
            w = WIDTH[comp[0]]
            start = jnp.where(last, rows - w, 0)
            source = take(given[comp[0]], comp, start, w)
            if comp[0] in HALF:
                target = messages.at[side, pl.ds(PLANE[comp], w)]
            elif comp[0] in ("lab", "gain"):
                target = ints.at[side, pl.ds(ints_at, w)]
                later.append((side, comp, ints, ints_at))
                ints_at += w
            else:
                target = floats.at[side, pl.ds(wide, w)]
                later.append((side, comp, floats, wide))
                wide += w
            started.append(pltpu.make_async_copy(source, target, sems.at[side, INDEX[comp]]))
    go(started)
    wait(tile_copies)
    from_first = (front_ref[...] == 1) == even_z

    def merge(y, carry):
        one, two = tile_in[0, y].astype(F32), tile_in[1, y].astype(F32)
        tiles[y] = jnp.where(from_first, one, two)
        return carry

    lax.fori_loop(0, rows, merge, 0)
    leaving = go([pltpu.make_async_copy(tiles, tile_out, other_sems.at[2])])
    for side in range(2):
        last = even if side == 0 else jnp.logical_not(even)
        corner = [jnp.where(last, tiles[rows - 3 + k], tiles[k]) for k in range(3)]
        messages[side, CORNERS] = jnp.concatenate(corner[:2], 1).astype(BF16)
        messages[side, CORNERS + 1] = jnp.concatenate([corner[2], corner[2]], 1).astype(BF16)
    wait(started)
    for side, comp, held, at in later:
        for k in range(WIDTH[comp[0]]):
            value = held[side, at + k].astype(F32)
            if comp[0] == "lab":
                value = value + 1.0
            messages[side, PLANE[comp] + k] = value.astype(BF16)
        if comp[0] == "Hs":
            last = even if side == 0 else jnp.logical_not(even)
            value = jnp.where(last, held[side, at + 1], held[side, at])
            low = value - value.astype(BF16).astype(F32)
            messages[side, LOW_BITS + comp[1]] = low.astype(BF16)
    leaving += go(
        [
            pltpu.make_async_copy(messages.at[side], outs[side], other_sems.at[3 + side])
            for side in range(2)
        ]
    )
    wait(leaving)


def pack_columns(*refs):
    given = dict(zip(NAMES, refs[: len(NAMES)]))
    first, second = refs[len(NAMES) :]
    even = lax.rem(lax.axis_index("gz"), 2) == 0
    lane = lane_of((8, 128))

    def some(block, carry):
        ys = [block * 4 + k for k in range(4)]
        low = [jnp.zeros((8, 128), F32) for y in ys]
        high = [jnp.zeros((8, 128), F32) for y in ys]
        for comp in reversed(COMPS):
            inside = lane < SPOT[comp] + WIDTH[comp[0]]
            for k, y in enumerate(ys):
                value = pull(given[comp[0]], comp, y)
                low[k] = jnp.where(inside, pltpu.roll(value[:, :128], SPOT[comp], 1), low[k])
                high[k] = jnp.where(inside, pltpu.roll(value[:, 128:], SPOT[comp], 1), high[k])
        for k, y in enumerate(ys):
            first[y] = jnp.where(even, high[k], low[k]).astype(BF16)
            second[y] = jnp.where(even, low[k], high[k]).astype(BF16)
        return carry

    lax.fori_loop(0, first.shape[0] // 4, some, 0)


def curl_ahead(v, above):
    inside = lax.broadcasted_iota(jnp.int32, v[0].shape, 0) < 7
    size = v[0].shape[1]

    def dz(c):
        return pltpu.roll(v[c], size - 1, 1) - v[c]

    def dx(c):
        return jnp.where(inside, pltpu.roll(v[c], 7, 0), 0.0) - v[c]

    return [
        (above[2] - v[2]) - dz(1),
        dz(0) - dx(2),
        dx(1) - (above[0] - v[0]),
    ]


def curl_back(v, below):
    inside = lax.broadcasted_iota(jnp.int32, v[0].shape, 0) > 0

    def dz(c):
        return v[c] - pltpu.roll(v[c], 1, 1)

    def dx(c):
        return v[c] - jnp.where(inside, pltpu.roll(v[c], 1, 0), 0.0)

    return [
        (v[2] - below[2]) - dz(1),
        dz(0) - dx(2),
        dx(1) - (v[0] - below[0]),
    ]


SCRATCH = dict(
    M=3, W=3, E1=3, Q1=3, F1=3, Q2=3, aE=3, aC=3, bH=3, cC=3, cE=3, hg=3, inv=1, g2=1, k0=1, k1=1
)


def six_stages(
    get, put, tally, held, bases, count, table, push_first, push_second, keep_row, keep_lane, flushes, arrivals
):
    def load(name, row):
        return [held[name][c, row] for c in range(SCRATCH[name])]

    def pair(name, row):
        return {0: held[name][0, row], 2: held[name][2, row]}

    def store(name, row, values):
        for c, value in enumerate(values):
            held[name][c, row] = value

    def kept(values, row):
        done = []
        for value in values:
            value = jnp.concatenate([value[:, :256], value[:, 256:] * keep_lane], 1)
            done.append(value if keep_row is None else value * keep_row(row))
        return done

    def trio(name, row):
        return [get((name, c), row) for c in range(3)]

    def stage_one(r):
        above = {0: get(("E", 0), r + 1), 2: get(("E", 2), r + 1)}
        curl = curl_ahead(trio("E", r), above)
        store("M", r, kept([h - 0.5 * c for h, c in zip(trio("H", r), curl)], r))

    def stage_two(r):
        electric, polar, rate = trio("E", r), trio("P", r), trio("Q", r)
        upper, lower = get(("N", 0), r), get(("N", 1), r)
        label, gain, source = get(("lab", 0), r), get(("gain", 0), r), get(("src", 0), r)
        inverse = jnp.zeros_like(label)
        for m, value in enumerate(table):
            inverse = jnp.where(label == m + 1.0, value, inverse)
        g2, g4 = 0.2 * gain, 0.4 * gain
        k0 = g4 * (upper - lower)
        q1 = [0.9 * q - 0.3 * p + k0 * e for q, p, e in zip(rate, polar, electric)]
        p1 = [p + 0.5 * q for p, q in zip(polar, q1)]
        curl = curl_back(load("M", r), pair("M", r - 1))
        f1 = [0.5 * (c - q) for c, q in zip(curl, q1)]
        f1[2] = f1[2] - push_first * source
        e1 = [e + inverse * f for e, f in zip(electric, f1)]
        s1 = g2 * sum(e * q for e, q in zip(e1, q1))
        up = upper + 0.5 * (0.05 * (1.0 - upper - lower) - 0.02 * upper)
        low = lower + 0.5 * (0.02 * upper - 0.3 * lower)
        k1 = g4 * (up - low - 2.0 * s1)
        q2 = [0.9 * q - 0.3 * p + k1 * e for q, p, e in zip(q1, p1, e1)]
        sb = g2 * (get(("Ns", 1), r) - get(("Ns", 0), r))
        a_e = [e + sb * q for e, q in zip(trio("Es", r), q2)]
        half = 0.5 * inverse
        store("E1", r, e1)
        store("Q1", r, q1)
        store("F1", r, f1)
        store("Q2", r, q2)
        store("aE", r, a_e)
        store("aC", r, [half * a for a in a_e])
        store("inv", r, [inverse])
        store("g2", r, [g2])
        store("k0", r, [k0])
        store("k1", r, [k1])

    def stage_three(r):
        curl = curl_ahead(load("E1", r), pair("E1", r + 1))
        store("W", r, kept([m - 0.5 * c for m, c in zip(load("M", r), curl)], r))
        curl = curl_ahead(load("aC", r), pair("aC", r + 1))
        store("bH", r, kept([h + c for h, c in zip(trio("Hs", r), curl)], r))

    def stage_four(r):
        (inverse,), (g2,), (k0,), (k1,) = load("inv", r), load("g2", r), load("k0", r), load("k1", r)
        up, low = get(("Ns", 0), r), get(("Ns", 1), r)
        sb = g2 * (low - up)
        curl = curl_back(load("W", r), pair("W", r - 1))
        q2, e1, a_e = load("Q2", r), load("E1", r), load("aE", r)
        f2 = [0.5 * (c - q) for c, q in zip(curl, q2)]
        f2[2] = f2[2] - push_second * get(("src", 0), r)
        e2 = [e + inverse * f for e, f in zip(e1, f2)]
        grad = sum(a[:, :256] * f[:, :256] for a, f in zip(a_e, f2))
        p_seed = trio("Ps", r)
        qt = [
            q + sb * e + 0.5 * (p - inverse * a)
            for q, e, p, a in zip(trio("Qs", r), e2, p_seed, a_e)
        ]
        dn = 2.0 * g2 * sum(q * e for q, e in zip(qt, e1))
        a_up = 0.965 * up + 0.01 * low + dn
        a_low = 0.85 * low - 0.025 * up - dn
        curl = curl_back(load("bH", r), pair("bH", r - 1))
        sb = g2 * (a_low - a_up)
        c_e = [
            a + k1 * q - 0.5 * c + sb * p for a, q, c, p in zip(a_e, qt, curl, load("Q1", r))
        ]
        half = 0.5 * inverse
        store("cC", r, [half * c for c in c_e])

        def own(value):
            return value[:, :256]

        grad = grad + sum(own(c) * own(f) for c, f in zip(c_e, load("F1", r)))
        inverse, g2, k0, sb = own(inverse), own(g2), own(k0), own(sb)
        p_out, q_out = [], []
        dn = 0.0
        for c in range(3):
            a_p = own(p_seed[c]) - 0.3 * own(qt[c])
            pt = a_p - inverse * own(c_e[c])
            q = 0.9 * own(qt[c]) + sb * own(e1[c]) + 0.5 * pt
            p_out.append(a_p - 0.3 * q)
            q_out.append(0.9 * q)
            dn = dn + q * own(get(("E", c), r))
            held["cE"][c, r] = own(c_e[c]) + k0 * q
        dn = 2.0 * g2 * dn
        a_up, a_low = own(a_up), own(a_low)
        put("polar", r, p_out)
        put("rate", r, q_out)
        put("levels", r, [0.965 * a_up + 0.01 * a_low + dn, 0.85 * a_low - 0.025 * a_up - dn])
        put("cell", r, [grad])

    def stage_five(r):
        curl = curl_ahead(load("cC", r), pair("cC", r + 1))
        store("hg", r, kept([h + c for h, c in zip(load("bH", r), curl)], r))

    def stage_six(r):
        hg = load("hg", r)
        curl = curl_back(hg, pair("hg", r - 1))
        put("h", r, [h[:, :256] for h in hg])
        put("e", r, [held["cE"][c, r] - 0.5 * curl[c][:, :256] for c in range(3)])
        tally(r)

    plan = (
        (stage_six, 7, 3, count - 3),
        (stage_five, 6, 2, count - 3),
        (stage_four, 4, 2, count - 2),
        (stage_three, 3, 1, count - 2),
        (stage_two, 1, 1, count - 1),
        (stage_one, 0, 0, count - 1),
    )
    marks = {low + lag for _, lag, low, high in plan} | {high + lag for _, lag, low, high in plan}
    marks = sorted(marks | {row + 7 for row in flushes})
    for begin, end in zip(marks, marks[1:]):
        active = [(f, lag) for f, lag, low, high in plan if low + lag <= begin and end <= high + lag]

        def body(i, carry, active=active):
            for f, lag in active:
                for base in bases:
                    f(i - lag + base)
            return carry

        if begin in arrivals:
            arrivals[begin]()
        if end - begin == 1:
            body(begin, 0)
        else:
            lax.fori_loop(begin, end, body, 0)
        if end - 7 in flushes:
            flushes[end - 7]()


OUTS = ("e", "h", "polar", "rate", "levels", "cell")
OUT_COMPS = dict(e=3, h=3, polar=3, rate=3, levels=2, cell=1)
HELD = tuple(SCRATCH)


def lane_keep():
    lane = lane_of((1, 128))
    outside = jnp.logical_and(lax.axis_index("gz") == 0, lane >= 64)
    return jnp.where(outside, 0.0, 1.0).astype(F32)


def material_sums(totals, label, value):
    for m in range(totals.shape[0]):
        totals[m] = totals[m] + jnp.where(label == m + 1.0, value, 0.0)


def leave(staged, outs, base, target, count, sems):
    copies = []
    for i, name in enumerate(OUTS):
        if OUT_COMPS[name] == 1:
            source = staged[name].at[0, pl.ds(base, count)]
            goal = outs[name].at[pl.ds(target, count)]
        else:
            source = staged[name].at[:, pl.ds(base, count)]
            goal = outs[name].at[:, pl.ds(target, count)]
        copies.append(pltpu.make_async_copy(source, goal, sems.at[i]))
    return go(copies)


def inner_kernel(rows, *refs):
    n = len(NAMES)
    sources = refs[: n + 1]
    table_ref, push_ref = refs[n + 1 : n + 3]
    at = n + 3
    outs = dict(zip(OUTS, refs[at : at + len(OUTS)]))
    totals = refs[at + len(OUTS)]
    at += len(OUTS) + 1
    inputs = refs[at : at + n + 1]
    given, tiles = dict(zip(NAMES, inputs[:n])), inputs[n]
    at += n + 1
    staged = dict(zip(OUTS, refs[at : at + len(OUTS)]))
    at += len(OUTS)
    held = dict(zip(HELD, refs[at : at + len(HELD)]))
    load_sems, sems = refs[at + len(HELD) :]

    arrivals = {}
    begins = {0: 0, 6: 7, 10: 11, 21: 22}
    bounds = list(begins.values()) + [rows]
    for piece, mark in enumerate(begins):
        low, high = bounds[piece], bounds[piece + 1]
        copies = []
        for i, (source, target) in enumerate(zip(sources, inputs)):
            where = pl.ds(low, high - low)
            if len(source.shape) == 4:
                source, target = source.at[:, where], target.at[:, where]
            else:
                source, target = source.at[where], target.at[where]
            copies.append(pltpu.make_async_copy(source, target, load_sems.at[piece, i]))
        go(copies)
        arrivals[mark] = lambda copies=copies: wait(copies)
    totals[...] = jnp.zeros_like(totals)

    def get(comp, r):
        third = pltpu.roll(tiles[r], 128 - SPOT[comp], 1)
        return jnp.concatenate([pull(given[comp[0]], comp, r), third], 1)

    def put(name, r, values):
        for c, value in enumerate(values):
            staged[name][c, r] = value

    def tally(r):
        material_sums(totals, given["lab"][r].astype(F32) + 1.0, staged["cell"][0, r])

    copies = []
    cuts = [3, 14, 22, rows - 3]

    def flush(piece):
        low, high = cuts[piece], cuts[piece + 1]
        copies.extend(leave(staged, outs, low, low, high - low, sems.at[piece]))

    flushes = {cuts[piece + 1]: (lambda piece=piece: flush(piece)) for piece in range(3)}
    six_stages(
        get,
        put,
        tally,
        held,
        (0,),
        rows,
        [table_ref[m] for m in range(table_ref.shape[0])],
        push_ref[0],
        push_ref[1],
        None,
        lane_keep(),
        flushes,
        arrivals,
    )
    wait(copies)


def edge_kernel(rows, scale, *refs):
    n = len(NAMES)
    given = dict(zip(NAMES, refs[:n]))
    tile_source, near, far, table_ref, push_ref, inner_totals = refs[n : n + 6]
    at = n + 6 + len(OUTS)
    outs = dict(zip(OUTS, refs[at : at + len(OUTS)]))
    sent = refs[at + len(OUTS)]
    at += len(OUTS) + 1
    raw = dict(zip(NAMES, refs[at : at + n]))
    tiles, halos, ext, totals = refs[at + n : at + n + 4]
    at += n + 4
    staged = dict(zip(OUTS, refs[at : at + len(OUTS)]))
    at += len(OUTS)
    held = dict(zip(HELD, refs[at : at + len(HELD)]))
    load_sems, halo_sems, sems = refs[at + len(HELD) :]
    even = lax.rem(lax.axis_index("gy"), 2) == 0
    top = lax.axis_index("gy") == 0

    def halo_copies(low, high):
        return [
            pltpu.make_async_copy(low, halos.at[0], halo_sems.at[0]),
            pltpu.make_async_copy(high, halos.at[1], halo_sems.at[1]),
        ]

    @pl.when(even)
    def _():
        go(halo_copies(far, near))

    @pl.when(jnp.logical_not(even))
    def _():
        go(halo_copies(near, far))

    copies = []
    for side in range(2):
        where, goal = pl.ds((0, rows - 6)[side], 6), pl.ds(side * 6, 6)
        for i, name in enumerate(NAMES):
            if COUNT[name] == 1:
                source, target = given[name].at[where], raw[name].at[goal]
            else:
                source, target = given[name].at[:, where], raw[name].at[:, goal]
            copies.append(pltpu.make_async_copy(source, target, load_sems.at[side, i]))
        copies.append(
            pltpu.make_async_copy(tile_source.at[where], tiles.at[goal], load_sems.at[side, n])
        )
    copies.append(pltpu.make_async_copy(inner_totals, totals, halo_sems.at[2]))
    go(copies)
    wait(halo_copies(near, far))
    for side in range(2):
        for comp in COMPS:
            w = WIDTH[comp[0]]
            for k in range(w):
                r = 3 - w + k if side == 0 else 6 + k
                main = halos[side, PLANE[comp] + k].astype(F32)
                if comp[0] == "Hs" and r == (2 if side == 0 else 6):
                    main = main + halos[side, LOW_BITS + comp[1]].astype(F32)
                t = r if side == 0 else r - 6
                tile = halos[side, CORNERS + t // 2].astype(F32)
                tile = tile[:, (t % 2) * 128 : (t % 2) * 128 + 128]
                third = pltpu.roll(tile, 128 - SPOT[comp], 1)
                ext[INDEX[comp], side * EDGE + r] = jnp.concatenate([main, third], 1)
    wait(copies)
    for side in range(2):
        for comp in COMPS:
            for k in range(6):
                r = 3 + k if side == 0 else k
                main = pull(raw[comp[0]], comp, side * 6 + k)
                third = pltpu.roll(tiles[side * 6 + k], 128 - SPOT[comp], 1)
                ext[INDEX[comp], side * EDGE + r] = jnp.concatenate([main, third], 1)

    def get(comp, r):
        return ext[INDEX[comp], r]

    def put(name, r, values):
        for c, value in enumerate(values):
            staged[name][c, r] = value

    def keep_row(r):
        return jnp.where(jnp.logical_and(top, r < 3), 0.0, 1.0).astype(F32)

    def tally(r):
        material_sums(totals, ext[INDEX[("lab", 0)], r, :, :256], staged["cell"][0, r])

    six_stages(
        get,
        put,
        tally,
        held,
        (0, EDGE),
        EDGE,
        [table_ref[m] for m in range(table_ref.shape[0])],
        push_ref[0],
        push_ref[1],
        keep_row,
        lane_keep(),
        {},
        {},
    )
    copies = []
    for side in range(2):
        start = 0 if side == 0 else rows - 3
        copies += leave(staged, outs, side * EDGE + 3, start, 3, sems.at[side])
    lane = lane_of((1, 128))
    line = jnp.zeros((1, 128), F32)
    for m in range(totals.shape[0]):
        line = jnp.where(lane == m, jnp.sum(totals[m]) * scale, line)
    sent[...] = jnp.broadcast_to(line[None], sent.shape)
    wait(copies)


def swapped(block, axes, odd):
    size = [lax.axis_size(a) for a in ("gy", "gz")]
    pairs = []
    for y in range(size[0]):
        for z in range(size[1]):
            y2, z2 = (y + 1, z) if axes == "gy" else (y, z + 1)
            at = y if axes == "gy" else z
            if at % 2 == odd and y2 < size[0] and z2 < size[1]:
                one, two = y * size[1] + z, y2 * size[1] + z2
                pairs += [(one, two), (two, one)]
    return lax.ppermute(block, ("gy", "gz"), pairs)


def on_device(
    efield_check,
    hfield_check,
    polar_check,
    rate_check,
    levels_check,
    efield_seed,
    hfield_seed,
    polar_seed,
    rate_seed,
    levels_seed,
    material_labels,
    gain_labels,
    inverse_table,
    source_field,
    start_step,
):
    given = (
        efield_check,
        hfield_check,
        polar_check,
        rate_check,
        levels_check,
        material_labels,
        gain_labels,
        source_field,
        efield_seed,
        levels_seed,
        hfield_seed,
        polar_seed,
        rate_seed,
    )
    rows = material_labels.shape[0]
    count = inverse_table.shape[0]
    start = start_step[0].astype(F32)
    pushes = jnp.stack([jnp.sin(SOURCE_OMEGA * start), jnp.sin(SOURCE_OMEGA * (start + 1.0))])
    hbm = pl.BlockSpec(memory_space=pltpu.HBM)
    anywhere = pl.BlockSpec(memory_space=pl.ANY)
    vmem = pl.BlockSpec(memory_space=pltpu.VMEM)
    smem = pl.BlockSpec(memory_space=pltpu.SMEM)
    limit = pltpu.CompilerParams(vmem_limit_bytes=60 * 1024 * 1024)
    tile_shape = jax.ShapeDtypeStruct((rows, 8, 128), BF16)
    blocks = 4

    def row_block(array):
        if array.ndim == 3:
            return pl.BlockSpec((rows // blocks, 8, 256), lambda i: (i, 0, 0))
        return pl.BlockSpec((array.shape[0], rows // blocks, 8, 256), lambda i: (0, i, 0, 0))

    tile_block = pl.BlockSpec((rows // blocks, 8, 128), lambda i: (i, 0, 0))
    send_first, send_second = pl.pallas_call(
        pack_columns,
        grid=(blocks,),
        out_shape=(tile_shape, tile_shape),
        in_specs=[row_block(array) for array in given],
        out_specs=(tile_block, tile_block),
        compiler_params=limit,
        name="pack_columns",
    )(*given)
    first = swapped(send_first, "gz", 0)
    second = swapped(send_second, "gz", 1)
    message = jax.ShapeDtypeStruct((PLANES, 8, 256), BF16)
    tiles, send_near, send_far = pl.pallas_call(
        lambda *refs: pack_rows(rows, *refs),
        out_shape=(jax.ShapeDtypeStruct((rows, 8, 128), F32), message, message),
        in_specs=[hbm] * len(given) + [anywhere, anywhere, vmem],
        out_specs=(anywhere, anywhere, anywhere),
        scratch_shapes=[
            pltpu.VMEM((2, PLANES, 8, 256), BF16),
            pltpu.VMEM((2, 24, 8, 256), F32),
            pltpu.VMEM((2, 4, 8, 256), jnp.int32),
            pltpu.VMEM((2, rows, 8, 128), BF16),
            pltpu.VMEM((rows, 8, 128), F32),
            pltpu.SemaphoreType.DMA((2, len(COMPS))),
            pltpu.SemaphoreType.DMA((5,)),
        ],
        compiler_params=limit,
        name="pack_rows",
    )(*given, first, second, jnp.broadcast_to(IS_FRONT, (8, 128)))
    far = swapped(send_far, "gy", 1)
    near = swapped(send_near, "gy", 0)

    def out_shape(name):
        dims = (rows, 8, 256)
        return jax.ShapeDtypeStruct(dims if OUT_COMPS[name] == 1 else (OUT_COMPS[name],) + dims, F32)

    def local(size):
        return [
            pltpu.VMEM((SCRATCH[name], size, 8, 256 if name == "cE" else LANES), F32)
            for name in HELD
        ]

    def copy_of(array, size):
        return pltpu.VMEM(array.shape[:-3] + (size,) + array.shape[-2:], array.dtype)

    sums = jax.ShapeDtypeStruct((count, 8, 256), F32)
    *inner, totals = pl.pallas_call(
        lambda *refs: inner_kernel(rows, *refs),
        out_shape=tuple(out_shape(name) for name in OUTS) + (sums,),
        in_specs=[hbm] * len(given) + [anywhere, smem, smem],
        out_specs=(hbm,) * len(OUTS) + (vmem,),
        scratch_shapes=[copy_of(array, rows) for array in (*given, tiles)]
        + [pltpu.VMEM((OUT_COMPS[name], rows, 8, 256), F32) for name in OUTS]
        + local(rows)
        + [
            pltpu.SemaphoreType.DMA((4, len(given) + 1)),
            pltpu.SemaphoreType.DMA((3, len(OUTS))),
        ],
        compiler_params=limit,
        cost_estimate=pl.CostEstimate(flops=40_000_000, bytes_accessed=12_000_000, transcendentals=0),
        name="inner_rows",
    )(*given, tiles, inverse_table, pushes)

    devices = lax.axis_size("gy") * lax.axis_size("gz")
    cells = rows * material_labels.shape[1] * material_labels.shape[2] * devices
    n = len(given) + 6
    *outs, sent = pl.pallas_call(
        lambda *refs: edge_kernel(rows, 1.0 / math.sqrt(cells), *refs),
        out_shape=tuple(out_shape(name) for name in OUTS)
        + (jax.ShapeDtypeStruct((devices, 1, 128), F32),),
        in_specs=[hbm] * len(given)
        + [anywhere] * 3
        + [smem, smem, anywhere]
        + [hbm] * len(OUTS),
        out_specs=(hbm,) * len(OUTS) + (vmem,),
        scratch_shapes=[copy_of(array, 12) for array in (*given, tiles)]
        + [
            pltpu.VMEM((2, PLANES, 8, 256), BF16),
            pltpu.VMEM((len(COMPS), 2 * EDGE, 8, LANES), F32),
            pltpu.VMEM((count, 8, 256), F32),
        ]
        + [pltpu.VMEM((OUT_COMPS[name], 2 * EDGE, 8, 256), F32) for name in OUTS]
        + local(2 * EDGE)
        + [
            pltpu.SemaphoreType.DMA((2, len(given) + 1)),
            pltpu.SemaphoreType.DMA((3,)),
            pltpu.SemaphoreType.DMA((2, len(OUTS))),
        ],
        input_output_aliases={n + i: i for i in range(len(OUTS))},
        compiler_params=limit,
        cost_estimate=pl.CostEstimate(flops=16_000_000, bytes_accessed=6_000_000, transcendentals=0),
        name="edge_rows",
    )(*given, tiles, near, far, inverse_table, pushes, totals, *inner)
    parts = lax.all_to_all(sent, ("gy", "gz"), 0, 0)
    table_grad = jnp.sum(parts[:, 0, :count], axis=0)
    return (*outs, table_grad)


def solution(mesh):
    field = P(None, "gy", None, "gz")
    cell = P("gy", None, "gz")
    return jax.shard_map(
        on_device,
        mesh=mesh,
        in_specs=(field,) * 10 + (cell, cell, P(), cell, P()),
        out_specs=(field,) * 5 + (cell, P()),
        check_vma=False,
    )
```

```python
import math

import jax
import jax.numpy as jnp
import numpy as np
from jax import lax
from jax.experimental import pallas as pl
from jax.experimental.pallas import tpu as pltpu
from jax.sharding import PartitionSpec as P


SOURCE_OMEGA = 0.35
F32 = jnp.float32
BF16 = jnp.bfloat16
NAMES = ("E", "H", "P", "Q", "N", "lab", "gain", "src", "Es", "Ns", "Hs", "Ps", "Qs")
COUNT = dict(E=3, H=3, P=3, Q=3, N=2, lab=1, gain=1, src=1, Es=3, Ns=2, Hs=3, Ps=3, Qs=3)
WIDTH = dict(E=3, H=3, P=2, Q=2, N=2, lab=2, gain=2, src=2, Es=2, Ns=2, Hs=2, Ps=1, Qs=1)
HALF = ("E", "H", "P", "Q", "N")
COMPS = [(name, c) for name in NAMES for c in range(COUNT[name])]
INDEX = {comp: i for i, comp in enumerate(COMPS)}
SPOT, PLANE, IS_FRONT = {}, {}, np.zeros((1, 128), np.int32)
_lane, _plane = 0, 0
for _comp in COMPS:
    _w = WIDTH[_comp[0]]
    SPOT[_comp] = _lane + _w
    IS_FRONT[0, _lane + _w : _lane + 2 * _w] = 1
    PLANE[_comp] = _plane
    _lane += 2 * _w
    _plane += _w
LOW_BITS = _plane
CORNERS = LOW_BITS + 3
PLANES = CORNERS + 2
LANES = 384
EDGE = 9


def lane_of(shape):
    return lax.broadcasted_iota(jnp.int32, shape, 1)


def go(copies):
    for copy in copies:
        copy.start()
    return copies


def wait(copies):
    for copy in copies:
        copy.wait()


def pull(ref, comp, index):
    name, c = comp
    if COUNT[name] == 1:
        value = ref[index].astype(F32)
        return value + 1.0 if name == "lab" else value
    return ref[c, index].astype(F32)


def take(ref, comp, start, count):
    if COUNT[comp[0]] == 1:
        return ref.at[pl.ds(start, count)]
    return ref.at[comp[1], pl.ds(start, count)]


def go(copies):
    for copy in copies:
        copy.start()
    return copies


def wait(copies):
    for copy in copies:
        copy.wait()


def front_lanes():
    lane = lane_of((8, 128))
    front = lane < 0
    for comp in COMPS:
        inside = jnp.logical_and(lane >= SPOT[comp], lane < SPOT[comp] + WIDTH[comp[0]])
        front = jnp.logical_or(front, inside)
    return front


def pack_kernel(rows, *refs):
    n = len(NAMES)
    given, whole = dict(zip(NAMES, refs[:n])), dict(zip(NAMES, refs[n : 2 * n]))
    first, second = refs[2 * n : 2 * n + 2]
    outs = refs[2 * n + 2 : 2 * n + 4]
    messages, floats, ints, sems, out_sems = refs[2 * n + 4 :]
    step = pl.program_id(0)
    even = lax.rem(lax.axis_index("gy"), 2) == 0
    copies, later = [], []
    for side in range(2):
        last = even if side == 0 else jnp.logical_not(even)
        wide = ints_at = 0
        for comp in COMPS:
            w = WIDTH[comp[0]]
            source = take(whole[comp[0]], comp, jnp.where(last, rows - w, 0), w)
            if comp[0] in HALF:
                target = messages.at[side, pl.ds(PLANE[comp], w)]
            elif comp[0] in ("lab", "gain"):
                target = ints.at[side, pl.ds(ints_at, w)]
                later.append((side, comp, ints, ints_at))
                ints_at += w
            else:
                target = floats.at[side, pl.ds(wide, w)]
                later.append((side, comp, floats, wide))
                wide += w
            copies.append(pltpu.make_async_copy(source, target, sems.at[side, INDEX[comp]]))
    leaving = [
        pltpu.make_async_copy(
            messages.at[side, pl.ds(0, CORNERS)], outs[side].at[pl.ds(0, CORNERS)], out_sems.at[side]
        )
        for side in range(2)
    ]

    @pl.when(step == 0)
    def _():
        go(copies)

    @pl.when(step == 1)
    def _():
        wait(copies)
        for side, comp, held, at in later:
            for k in range(WIDTH[comp[0]]):
                value = held[side, at + k].astype(F32)
                if comp[0] == "lab":
                    value = value + 1.0
                messages[side, PLANE[comp] + k] = value.astype(BF16)
            if comp[0] == "Hs":
                last = even if side == 0 else jnp.logical_not(even)
                value = jnp.where(last, held[side, at + 1], held[side, at])
                low = value - value.astype(BF16).astype(F32)
                messages[side, LOW_BITS + comp[1]] = low.astype(BF16)
        go(leaving)

    even_z = lax.rem(lax.axis_index("gz"), 2) == 0
    lane = lane_of((8, 128))

    def some(block, carry):
        ys = [block * 4 + k for k in range(4)]
        low = [jnp.zeros((8, 128), F32) for y in ys]
        high = [jnp.zeros((8, 128), F32) for y in ys]
        for comp in reversed(COMPS):
            inside = lane < SPOT[comp] + WIDTH[comp[0]]
            for k, y in enumerate(ys):
                value = pull(given[comp[0]], comp, y)
                low[k] = jnp.where(inside, pltpu.roll(value[:, :128], SPOT[comp], 1), low[k])
                high[k] = jnp.where(inside, pltpu.roll(value[:, 128:], SPOT[comp], 1), high[k])
        for k, y in enumerate(ys):
            first[y] = jnp.where(even_z, high[k], low[k]).astype(BF16)
            second[y] = jnp.where(even_z, low[k], high[k]).astype(BF16)
        return carry

    lax.fori_loop(0, first.shape[0] // 4, some, 0)

    @pl.when(step == pl.num_programs(0) - 1)
    def _():
        wait(leaving)


def corner_kernel(rows, first, second, pushes, *refs):
    tiles, outs = refs[2], refs[3:5]
    corners, sems = refs[5:]
    even = lax.rem(lax.axis_index("gy"), 2) == 0
    even_z = lax.rem(lax.axis_index("gz"), 2) == 0
    from_first = front_lanes() == even_z

    def merge(y):
        tiles[y] = jnp.where(from_first, first[y].astype(F32), second[y].astype(F32))

    ends = list(range(3)) + list(range(rows - 3, rows))
    for y in ends:
        merge(y)
    for side in range(2):
        last = even if side == 0 else jnp.logical_not(even)
        corner = [jnp.where(last, tiles[rows - 3 + k], tiles[k]) for k in range(3)]
        corners[side, 0] = jnp.concatenate(corner[:2], 1).astype(BF16)
        corners[side, 1] = jnp.concatenate([corner[2], corner[2]], 1).astype(BF16)
    copies = go(
        [
            pltpu.make_async_copy(
                corners.at[side], outs[side].at[pl.ds(CORNERS, 2)], sems.at[side]
            )
            for side in range(2)
        ]
    )
    for y in range(3, rows - 3):
        merge(y)
    wait(copies)


def curl_ahead(v, above):
    inside = lax.broadcasted_iota(jnp.int32, v[0].shape, 0) < 7
    size = v[0].shape[1]

    def dz(c):
        return pltpu.roll(v[c], size - 1, 1) - v[c]

    def dx(c):
        return jnp.where(inside, pltpu.roll(v[c], 7, 0), 0.0) - v[c]

    return [
        (above[2] - v[2]) - dz(1),
        dz(0) - dx(2),
        dx(1) - (above[0] - v[0]),
    ]


def curl_back(v, below):
    inside = lax.broadcasted_iota(jnp.int32, v[0].shape, 0) > 0

    def dz(c):
        return v[c] - pltpu.roll(v[c], 1, 1)

    def dx(c):
        return v[c] - jnp.where(inside, pltpu.roll(v[c], 1, 0), 0.0)

    return [
        (v[2] - below[2]) - dz(1),
        dz(0) - dx(2),
        dx(1) - (v[0] - below[0]),
    ]


SCRATCH = dict(
    M=3, W=3, E1=3, Q1=3, F1=3, Q2=3, aE=3, aC=3, bH=3, cC=3, cE=3, hg=3, inv=1, g2=1, k0=1, k1=1
)


def six_stages(
    get, put, tally, held, bases, count, table, push_first, push_second, keep_row, keep_lane, flushes, arrivals
):
    def load(name, row):
        return [held[name][c, row] for c in range(SCRATCH[name])]

    def pair(name, row):
        return {0: held[name][0, row], 2: held[name][2, row]}

    def store(name, row, values):
        for c, value in enumerate(values):
            held[name][c, row] = value

    def kept(values, row):
        done = []
        for value in values:
            value = jnp.concatenate([value[:, :256], value[:, 256:] * keep_lane], 1)
            done.append(value if keep_row is None else value * keep_row(row))
        return done

    def trio(name, row):
        return [get((name, c), row) for c in range(3)]

    def stage_one(r):
        above = {0: get(("E", 0), r + 1), 2: get(("E", 2), r + 1)}
        curl = curl_ahead(trio("E", r), above)
        store("M", r, kept([h - 0.5 * c for h, c in zip(trio("H", r), curl)], r))

    def stage_two(r):
        electric, polar, rate = trio("E", r), trio("P", r), trio("Q", r)
        upper, lower = get(("N", 0), r), get(("N", 1), r)
        label, gain, source = get(("lab", 0), r), get(("gain", 0), r), get(("src", 0), r)
        inverse = jnp.zeros_like(label)
        for m, value in enumerate(table):
            inverse = jnp.where(label == m + 1.0, value, inverse)
        g2, g4 = 0.2 * gain, 0.4 * gain
        k0 = g4 * (upper - lower)
        q1 = [0.9 * q - 0.3 * p + k0 * e for q, p, e in zip(rate, polar, electric)]
        p1 = [p + 0.5 * q for p, q in zip(polar, q1)]
        curl = curl_back(load("M", r), pair("M", r - 1))
        f1 = [0.5 * (c - q) for c, q in zip(curl, q1)]
        f1[2] = f1[2] - push_first * source
        e1 = [e + inverse * f for e, f in zip(electric, f1)]
        s1 = g2 * sum(e * q for e, q in zip(e1, q1))
        up = upper + 0.5 * (0.05 * (1.0 - upper - lower) - 0.02 * upper)
        low = lower + 0.5 * (0.02 * upper - 0.3 * lower)
        k1 = g4 * (up - low - 2.0 * s1)
        q2 = [0.9 * q - 0.3 * p + k1 * e for q, p, e in zip(q1, p1, e1)]
        sb = g2 * (get(("Ns", 1), r) - get(("Ns", 0), r))
        a_e = [e + sb * q for e, q in zip(trio("Es", r), q2)]
        half = 0.5 * inverse
        store("E1", r, e1)
        store("Q1", r, q1)
        store("F1", r, f1)
        store("Q2", r, q2)
        store("aE", r, a_e)
        store("aC", r, [half * a for a in a_e])
        store("inv", r, [inverse])
        store("g2", r, [g2])
        store("k0", r, [k0])
        store("k1", r, [k1])

    def stage_three(r):
        curl = curl_ahead(load("E1", r), pair("E1", r + 1))
        store("W", r, kept([m - 0.5 * c for m, c in zip(load("M", r), curl)], r))
        curl = curl_ahead(load("aC", r), pair("aC", r + 1))
        store("bH", r, kept([h + c for h, c in zip(trio("Hs", r), curl)], r))

    def stage_four(r):
        (inverse,), (g2,), (k0,), (k1,) = load("inv", r), load("g2", r), load("k0", r), load("k1", r)
        up, low = get(("Ns", 0), r), get(("Ns", 1), r)
        sb = g2 * (low - up)
        curl = curl_back(load("W", r), pair("W", r - 1))
        q2, e1, a_e = load("Q2", r), load("E1", r), load("aE", r)
        f2 = [0.5 * (c - q) for c, q in zip(curl, q2)]
        f2[2] = f2[2] - push_second * get(("src", 0), r)
        e2 = [e + inverse * f for e, f in zip(e1, f2)]
        grad = sum(a[:, :256] * f[:, :256] for a, f in zip(a_e, f2))
        p_seed = trio("Ps", r)
        qt = [
            q + sb * e + 0.5 * (p - inverse * a)
            for q, e, p, a in zip(trio("Qs", r), e2, p_seed, a_e)
        ]
        dn = 2.0 * g2 * sum(q * e for q, e in zip(qt, e1))
        a_up = 0.965 * up + 0.01 * low + dn
        a_low = 0.85 * low - 0.025 * up - dn
        curl = curl_back(load("bH", r), pair("bH", r - 1))
        sb = g2 * (a_low - a_up)
        c_e = [
            a + k1 * q - 0.5 * c + sb * p for a, q, c, p in zip(a_e, qt, curl, load("Q1", r))
        ]
        half = 0.5 * inverse
        store("cC", r, [half * c for c in c_e])

        def own(value):
            return value[:, :256]

        grad = grad + sum(own(c) * own(f) for c, f in zip(c_e, load("F1", r)))
        inverse, g2, k0, sb = own(inverse), own(g2), own(k0), own(sb)
        p_out, q_out = [], []
        dn = 0.0
        for c in range(3):
            a_p = own(p_seed[c]) - 0.3 * own(qt[c])
            pt = a_p - inverse * own(c_e[c])
            q = 0.9 * own(qt[c]) + sb * own(e1[c]) + 0.5 * pt
            p_out.append(a_p - 0.3 * q)
            q_out.append(0.9 * q)
            dn = dn + q * own(get(("E", c), r))
            held["cE"][c, r] = own(c_e[c]) + k0 * q
        dn = 2.0 * g2 * dn
        a_up, a_low = own(a_up), own(a_low)
        put("polar", r, p_out)
        put("rate", r, q_out)
        put("levels", r, [0.965 * a_up + 0.01 * a_low + dn, 0.85 * a_low - 0.025 * a_up - dn])
        put("cell", r, [grad])

    def stage_five(r):
        curl = curl_ahead(load("cC", r), pair("cC", r + 1))
        store("hg", r, kept([h + c for h, c in zip(load("bH", r), curl)], r))

    def stage_six(r):
        hg = load("hg", r)
        curl = curl_back(hg, pair("hg", r - 1))
        put("h", r, [h[:, :256] for h in hg])
        put("e", r, [held["cE"][c, r] - 0.5 * curl[c][:, :256] for c in range(3)])
        tally(r)

    plan = (
        (stage_six, 7, 3, count - 3),
        (stage_five, 6, 2, count - 3),
        (stage_four, 4, 2, count - 2),
        (stage_three, 3, 1, count - 2),
        (stage_two, 1, 1, count - 1),
        (stage_one, 0, 0, count - 1),
    )
    marks = {low + lag for _, lag, low, high in plan} | {high + lag for _, lag, low, high in plan}
    marks = sorted(marks | {row + 7 for row in flushes})
    for begin, end in zip(marks, marks[1:]):
        active = [(f, lag) for f, lag, low, high in plan if low + lag <= begin and end <= high + lag]

        def body(i, carry, active=active):
            for f, lag in active:
                for base in bases:
                    f(i - lag + base)
            return carry

        if begin in arrivals:
            arrivals[begin]()
        if end - begin == 1:
            body(begin, 0)
        else:
            lax.fori_loop(begin, end, body, 0)
        if end - 7 in flushes:
            flushes[end - 7]()


OUTS = ("e", "h", "polar", "rate", "levels", "cell")
OUT_COMPS = dict(e=3, h=3, polar=3, rate=3, levels=2, cell=1)
HELD = tuple(SCRATCH)


def lane_keep():
    lane = lane_of((1, 128))
    outside = jnp.logical_and(lax.axis_index("gz") == 0, lane >= 64)
    return jnp.where(outside, 0.0, 1.0).astype(F32)


def material_sums(totals, label, value):
    for m in range(totals.shape[0]):
        totals[m] = totals[m] + jnp.where(label == m + 1.0, value, 0.0)


def leave(staged, outs, base, target, count, sems):
    copies = []
    for i, name in enumerate(OUTS):
        if OUT_COMPS[name] == 1:
            source = staged[name].at[0, pl.ds(base, count)]
            goal = outs[name].at[pl.ds(target, count)]
        else:
            source = staged[name].at[:, pl.ds(base, count)]
            goal = outs[name].at[:, pl.ds(target, count)]
        copies.append(pltpu.make_async_copy(source, goal, sems.at[i]))
    return go(copies)


def inner_kernel(rows, *refs):
    n = len(NAMES)
    sources = refs[: n + 1]
    table_ref, push_ref = refs[n + 1 : n + 3]
    at = n + 3
    outs = dict(zip(OUTS, refs[at : at + len(OUTS)]))
    totals, ext = refs[at + len(OUTS) : at + len(OUTS) + 2]
    at += len(OUTS) + 2
    inputs = refs[at : at + n + 1]
    given, tiles = dict(zip(NAMES, inputs[:n])), inputs[n]
    at += n + 1
    staged = dict(zip(OUTS, refs[at : at + len(OUTS)]))
    at += len(OUTS)
    held = dict(zip(HELD, refs[at : at + len(HELD)]))
    load_sems, sems = refs[at + len(HELD) :]

    arrivals = {}
    begins = {0: 0, 6: 7, 10: 11, 21: 22}
    bounds = list(begins.values()) + [rows]
    for piece, mark in enumerate(begins):
        low, high = bounds[piece], bounds[piece + 1]
        copies = []
        for i, (source, target) in enumerate(zip(sources, inputs)):
            where = pl.ds(low, high - low)
            if len(source.shape) == 4:
                source, target = source.at[:, where], target.at[:, where]
            else:
                source, target = source.at[where], target.at[where]
            copies.append(pltpu.make_async_copy(source, target, load_sems.at[piece, i]))
        go(copies)
        arrivals[mark] = lambda copies=copies: wait(copies)
    totals[...] = jnp.zeros_like(totals)

    def get(comp, r):
        third = pltpu.roll(tiles[r], 128 - SPOT[comp], 1)
        return jnp.concatenate([pull(given[comp[0]], comp, r), third], 1)

    def put(name, r, values):
        for c, value in enumerate(values):
            staged[name][c, r] = value

    def tally(r):
        material_sums(totals, given["lab"][r].astype(F32) + 1.0, staged["cell"][0, r])

    copies = []
    cuts = [3, 14, 22, rows - 3]

    def flush(piece):
        low, high = cuts[piece], cuts[piece + 1]
        copies.extend(leave(staged, outs, low, low, high - low, sems.at[piece]))

    flushes = {cuts[piece + 1]: (lambda piece=piece: flush(piece)) for piece in range(3)}
    six_stages(
        get,
        put,
        tally,
        held,
        (0,),
        rows,
        [table_ref[m] for m in range(table_ref.shape[0])],
        push_ref[0],
        push_ref[1],
        None,
        lane_keep(),
        flushes,
        arrivals,
    )

    def hand_on(k, carry):
        for comp in COMPS:
            ext[INDEX[comp], k] = get(comp, k)
            ext[INDEX[comp], 6 + k] = get(comp, rows - 6 + k)
        return carry

    lax.fori_loop(0, 6, hand_on, 0)
    wait(copies)


def edge_kernel(rows, scale, near, far, own, inner_totals, table_ref, push_ref, *refs):
    outs = dict(zip(OUTS, refs[len(OUTS) : 2 * len(OUTS)]))
    sent, ext, totals = refs[2 * len(OUTS) : 2 * len(OUTS) + 3]
    at = 2 * len(OUTS) + 3
    staged = dict(zip(OUTS, refs[at : at + len(OUTS)]))
    at += len(OUTS)
    held = dict(zip(HELD, refs[at : at + len(HELD)]))
    sems = refs[at + len(HELD)]
    even = lax.rem(lax.axis_index("gy"), 2) == 0
    top = lax.axis_index("gy") == 0
    totals[...] = inner_totals[...]

    def arrived(side, plane):
        use_far = even if side == 0 else jnp.logical_not(even)
        return jnp.where(use_far, far[plane].astype(F32), near[plane].astype(F32))

    for side in range(2):
        tiles = []
        for t in range(3):
            tile = arrived(side, CORNERS + t // 2)
            tiles.append(tile[:, (t % 2) * 128 : (t % 2) * 128 + 128])
        for comp in COMPS:
            w = WIDTH[comp[0]]
            for k in range(w):
                r = 3 - w + k if side == 0 else 6 + k
                main = arrived(side, PLANE[comp] + k)
                if comp[0] == "Hs" and r == (2 if side == 0 else 6):
                    main = main + arrived(side, LOW_BITS + comp[1])
                third = pltpu.roll(tiles[r if side == 0 else r - 6], 128 - SPOT[comp], 1)
                ext[INDEX[comp], side * EDGE + r] = jnp.concatenate([main, third], 1)

    def bring(k, carry):
        for comp in COMPS:
            ext[INDEX[comp], 3 + k] = own[INDEX[comp], k]
        return carry

    lax.fori_loop(0, 12, bring, 0)

    def get(comp, r):
        return ext[INDEX[comp], r]

    def put(name, r, values):
        for c, value in enumerate(values):
            staged[name][c, r] = value

    def keep_row(r):
        return jnp.where(jnp.logical_and(top, r < 3), 0.0, 1.0).astype(F32)

    def tally(r):
        material_sums(totals, ext[INDEX[("lab", 0)], r, :, :256], staged["cell"][0, r])

    six_stages(
        get,
        put,
        tally,
        held,
        (0, EDGE),
        EDGE,
        [table_ref[m] for m in range(table_ref.shape[0])],
        push_ref[0],
        push_ref[1],
        keep_row,
        lane_keep(),
        {},
        {},
    )
    copies = []
    for side in range(2):
        start = 0 if side == 0 else rows - 3
        copies += leave(staged, outs, side * EDGE + 3, start, 3, sems.at[side])
    lane = lane_of((1, 128))
    line = jnp.zeros((1, 128), F32)
    for m in range(totals.shape[0]):
        line = jnp.where(lane == m, jnp.sum(totals[m]) * scale, line)
    sent[...] = jnp.broadcast_to(line[None], sent.shape)
    wait(copies)


def swapped(block, axes, odd):
    size = [lax.axis_size(a) for a in ("gy", "gz")]
    pairs = []
    for y in range(size[0]):
        for z in range(size[1]):
            y2, z2 = (y + 1, z) if axes == "gy" else (y, z + 1)
            at = y if axes == "gy" else z
            if at % 2 == odd and y2 < size[0] and z2 < size[1]:
                one, two = y * size[1] + z, y2 * size[1] + z2
                pairs += [(one, two), (two, one)]
    return lax.ppermute(block, ("gy", "gz"), pairs)


def on_device(
    efield_check,
    hfield_check,
    polar_check,
    rate_check,
    levels_check,
    efield_seed,
    hfield_seed,
    polar_seed,
    rate_seed,
    levels_seed,
    material_labels,
    gain_labels,
    inverse_table,
    source_field,
    start_step,
):
    given = (
        efield_check,
        hfield_check,
        polar_check,
        rate_check,
        levels_check,
        material_labels,
        gain_labels,
        source_field,
        efield_seed,
        levels_seed,
        hfield_seed,
        polar_seed,
        rate_seed,
    )
    fixed = [pltpu.with_memory_space_constraint(array, pltpu.HBM) for array in given]
    rows = material_labels.shape[0]
    count = inverse_table.shape[0]
    start = start_step[0].astype(F32)
    pushes = jnp.stack([jnp.sin(SOURCE_OMEGA * start), jnp.sin(SOURCE_OMEGA * (start + 1.0))])
    hbm = pl.BlockSpec(memory_space=pltpu.HBM)
    anywhere = pl.BlockSpec(memory_space=pl.ANY)
    vmem = pl.BlockSpec(memory_space=pltpu.VMEM)
    smem = pl.BlockSpec(memory_space=pltpu.SMEM)
    tile_shape = jax.ShapeDtypeStruct((rows, 8, 128), BF16)
    message = jax.ShapeDtypeStruct((PLANES, 8, 256), BF16)
    blocks = 4

    def row_block(array):
        if array.ndim == 3:
            return pl.BlockSpec((rows // blocks, 8, 256), lambda i: (i, 0, 0))
        return pl.BlockSpec((array.shape[0], rows // blocks, 8, 256), lambda i: (0, i, 0, 0))

    def grant(mib):
        return pltpu.CompilerParams(vmem_limit_bytes=mib * 1024 * 1024)

    tile_block = pl.BlockSpec((rows // blocks, 8, 128), lambda i: (i, 0, 0))
    send_first, send_second, send_near, send_far = pl.pallas_call(
        lambda *refs: pack_kernel(rows, *refs),
        grid=(blocks,),
        out_shape=(tile_shape, tile_shape, message, message),
        in_specs=[row_block(array) for array in given] + [hbm] * len(given),
        out_specs=(tile_block, tile_block, hbm, hbm),
        scratch_shapes=[
            pltpu.VMEM((2, PLANES, 8, 256), BF16),
            pltpu.VMEM((2, 24, 8, 256), F32),
            pltpu.VMEM((2, 4, 8, 256), jnp.int32),
            pltpu.SemaphoreType.DMA((2, len(COMPS))),
            pltpu.SemaphoreType.DMA((2,)),
        ],
        compiler_params=grant(60),
        name="pack_kernel",
    )(*given, *given)
    first = swapped(send_first, "gz", 0)
    second = swapped(send_second, "gz", 1)
    tiles, send_near, send_far = pl.pallas_call(
        lambda *refs: corner_kernel(rows, *refs),
        out_shape=(jax.ShapeDtypeStruct((rows, 8, 128), F32), message, message),
        in_specs=[vmem, vmem, smem, hbm, hbm],
        out_specs=(vmem, hbm, hbm),
        scratch_shapes=[
            pltpu.VMEM((2, 2, 8, 256), BF16),
            pltpu.SemaphoreType.DMA((2,)),
        ],
        input_output_aliases={3: 1, 4: 2},
        compiler_params=grant(4),
        name="corner_kernel",
    )(first, second, pushes, send_near, send_far)
    far = swapped(send_far, "gy", 1)
    near = swapped(send_near, "gy", 0)

    def out_shape(name):
        dims = (rows, 8, 256)
        return jax.ShapeDtypeStruct(dims if OUT_COMPS[name] == 1 else (OUT_COMPS[name],) + dims, F32)

    def local(size):
        return [
            pltpu.VMEM((SCRATCH[name], size, 8, 256 if name == "cE" else LANES), F32)
            for name in HELD
        ]

    def copy_of(array, size):
        return pltpu.VMEM(array.shape[:-3] + (size,) + array.shape[-2:], array.dtype)

    sums = jax.ShapeDtypeStruct((count, 8, 256), F32)
    handed = jax.ShapeDtypeStruct((len(COMPS), 12, 8, LANES), F32)
    *inner, totals, own = pl.pallas_call(
        lambda *refs: inner_kernel(rows, *refs),
        out_shape=tuple(out_shape(name) for name in OUTS) + (sums, handed),
        in_specs=[hbm] * len(given) + [anywhere, smem, smem],
        out_specs=(hbm,) * len(OUTS) + (vmem, vmem),
        scratch_shapes=[copy_of(array, rows) for array in (*given, tiles)]
        + [pltpu.VMEM((OUT_COMPS[name], rows, 8, 256), F32) for name in OUTS]
        + local(rows)
        + [
            pltpu.SemaphoreType.DMA((4, len(given) + 1)),
            pltpu.SemaphoreType.DMA((3, len(OUTS))),
        ],
        compiler_params=grant(32),
        cost_estimate=pl.CostEstimate(flops=40_000_000, bytes_accessed=12_000_000, transcendentals=0),
        name="inner_rows",
    )(*fixed, tiles, inverse_table, pushes)

    devices = lax.axis_size("gy") * lax.axis_size("gz")
    cells = rows * material_labels.shape[1] * material_labels.shape[2] * devices
    *outs, sent = pl.pallas_call(
        lambda *refs: edge_kernel(rows, 1.0 / math.sqrt(cells), *refs),
        out_shape=tuple(out_shape(name) for name in OUTS)
        + (jax.ShapeDtypeStruct((devices, 1, 128), F32),),
        in_specs=[vmem] * 4 + [smem, smem] + [hbm] * len(OUTS),
        out_specs=(hbm,) * len(OUTS) + (vmem,),
        scratch_shapes=[
            pltpu.VMEM((len(COMPS), 2 * EDGE, 8, LANES), F32),
            pltpu.VMEM((count, 8, 256), F32),
        ]
        + [pltpu.VMEM((OUT_COMPS[name], 2 * EDGE, 8, 256), F32) for name in OUTS]
        + local(2 * EDGE)
        + [pltpu.SemaphoreType.DMA((2, len(OUTS)))],
        input_output_aliases={6 + i: i for i in range(len(OUTS))},
        compiler_params=grant(26),
        cost_estimate=pl.CostEstimate(flops=16_000_000, bytes_accessed=6_000_000, transcendentals=0),
        name="edge_rows",
    )(near, far, own, totals, inverse_table, pushes, *inner)
    parts = lax.all_to_all(sent, ("gy", "gz"), 0, 0)
    table_grad = jnp.sum(parts[:, 0, :count], axis=0)
    return (*outs, table_grad)


def solution(mesh):
    field = P(None, "gy", None, "gz")
    cell = P("gy", None, "gz")
    return jax.shard_map(
        on_device,
        mesh=mesh,
        in_specs=(field,) * 10 + (cell, cell, P(), cell, P()),
        out_specs=(field,) * 5 + (cell, P()),
        check_vma=False,
    )
```

```python
import math

import jax
import jax.numpy as jnp
import numpy as np
from jax import lax
from jax.experimental import pallas as pl
from jax.experimental.pallas import tpu as pltpu
from jax.sharding import PartitionSpec as P


SOURCE_OMEGA = 0.35
F32 = jnp.float32
BF16 = jnp.bfloat16
NAMES = ("E", "H", "P", "Q", "N", "lab", "gain", "src", "Es", "Ns", "Hs", "Ps", "Qs")
COUNT = dict(E=3, H=3, P=3, Q=3, N=2, lab=1, gain=1, src=1, Es=3, Ns=2, Hs=3, Ps=3, Qs=3)
WIDTH = dict(E=3, H=3, P=2, Q=2, N=2, lab=2, gain=2, src=2, Es=2, Ns=2, Hs=2, Ps=1, Qs=1)
HALF = ("E", "H", "P", "Q", "N")
COMPS = [(name, c) for name in NAMES for c in range(COUNT[name])]
INDEX = {comp: i for i, comp in enumerate(COMPS)}
SPOT, PLANE, IS_FRONT = {}, {}, np.zeros((1, 128), np.int32)
_lane, _plane = 0, 0
for _comp in COMPS:
    _w = WIDTH[_comp[0]]
    SPOT[_comp] = _lane + _w
    IS_FRONT[0, _lane + _w : _lane + 2 * _w] = 1
    PLANE[_comp] = _plane
    _lane += 2 * _w
    _plane += _w
LOW_BITS = _plane
CORNERS = LOW_BITS + 3
PLANES = CORNERS + 2
LANES = 384
EDGE = 9


def lane_of(shape):
    return lax.broadcasted_iota(jnp.int32, shape, 1)


def go(copies):
    for copy in copies:
        copy.start()
    return copies


def wait(copies):
    for copy in copies:
        copy.wait()


def pull(ref, comp, index):
    name, c = comp
    if COUNT[name] == 1:
        value = ref[index].astype(F32)
        return value + 1.0 if name == "lab" else value
    return ref[c, index].astype(F32)


def take(ref, comp, start, count):
    if COUNT[comp[0]] == 1:
        return ref.at[pl.ds(start, count)]
    return ref.at[comp[1], pl.ds(start, count)]


def go(copies):
    for copy in copies:
        copy.start()
    return copies


def wait(copies):
    for copy in copies:
        copy.wait()


def front_lanes():
    lane = lane_of((8, 128))
    front = lane < 0
    for comp in COMPS:
        inside = jnp.logical_and(lane >= SPOT[comp], lane < SPOT[comp] + WIDTH[comp[0]])
        front = jnp.logical_or(front, inside)
    return front


def pack_kernel(rows, *refs):
    n = len(NAMES)
    given, whole = dict(zip(NAMES, refs[:n])), dict(zip(NAMES, refs[n : 2 * n]))
    edges, *outs = refs[2 * n : 2 * n + 3]
    messages, floats, ints, sems, out_sems = refs[2 * n + 3 :]
    step = pl.program_id(0)
    even = lax.rem(lax.axis_index("gy"), 2) == 0
    copies, later = [], []
    for side in range(2):
        last = even if side == 0 else jnp.logical_not(even)
        wide = ints_at = 0
        for comp in COMPS:
            w = WIDTH[comp[0]]
            source = take(whole[comp[0]], comp, jnp.where(last, rows - w, 0), w)
            if comp[0] in HALF:
                target = messages.at[side, pl.ds(PLANE[comp], w)]
            elif comp[0] in ("lab", "gain"):
                target = ints.at[side, pl.ds(ints_at, w)]
                later.append((side, comp, ints, ints_at))
                ints_at += w
            else:
                target = floats.at[side, pl.ds(wide, w)]
                later.append((side, comp, floats, wide))
                wide += w
            copies.append(pltpu.make_async_copy(source, target, sems.at[side, INDEX[comp]]))
    leaving = [
        pltpu.make_async_copy(
            messages.at[side, pl.ds(0, CORNERS)], outs[side].at[pl.ds(0, CORNERS)], out_sems.at[side]
        )
        for side in range(2)
    ]

    @pl.when(step == 0)
    def _():
        go(copies)

    @pl.when(step == 1)
    def _():
        wait(copies)
        for side, comp, held, at in later:
            for k in range(WIDTH[comp[0]]):
                value = held[side, at + k].astype(F32)
                if comp[0] == "lab":
                    value = value + 1.0
                messages[side, PLANE[comp] + k] = value.astype(BF16)
            if comp[0] == "Hs":
                last = even if side == 0 else jnp.logical_not(even)
                value = jnp.where(last, held[side, at + 1], held[side, at])
                low = value - value.astype(BF16).astype(F32)
                messages[side, LOW_BITS + comp[1]] = low.astype(BF16)
        go(leaving)

    lane = lane_of((8, 128))

    def some(block, carry):
        ys = [block * 4 + k for k in range(4)]
        packed = [jnp.zeros((8, 128), F32) for y in ys]
        for comp in reversed(COMPS):
            inside = lane < SPOT[comp] + WIDTH[comp[0]]
            for k, y in enumerate(ys):
                value = pull(given[comp[0]], comp, y)
                value = jnp.where(lane < 64, value[:, :128], value[:, 128:])
                packed[k] = jnp.where(inside, pltpu.roll(value, SPOT[comp], 1), packed[k])
        for k, y in enumerate(ys):
            edges[y] = packed[k].astype(BF16)
        return carry

    lax.fori_loop(0, edges.shape[0] // 4, some, 0)

    @pl.when(step == pl.num_programs(0) - 1)
    def _():
        wait(leaving)


def corner_kernel(rows, first, second, pushes, *refs):
    tiles, outs = refs[2], refs[3:5]
    corners, sems = refs[5:]
    even = lax.rem(lax.axis_index("gy"), 2) == 0
    even_z = lax.rem(lax.axis_index("gz"), 2) == 0
    from_first = front_lanes() == even_z

    def merge(y):
        tiles[y] = jnp.where(from_first, first[y].astype(F32), second[y].astype(F32))

    ends = list(range(3)) + list(range(rows - 3, rows))
    for y in ends:
        merge(y)
    for side in range(2):
        last = even if side == 0 else jnp.logical_not(even)
        corner = [jnp.where(last, tiles[rows - 3 + k], tiles[k]) for k in range(3)]
        corners[side, 0] = jnp.concatenate(corner[:2], 1).astype(BF16)
        corners[side, 1] = jnp.concatenate([corner[2], corner[2]], 1).astype(BF16)
    copies = go(
        [
            pltpu.make_async_copy(
                corners.at[side], outs[side].at[pl.ds(CORNERS, 2)], sems.at[side]
            )
            for side in range(2)
        ]
    )
    for y in range(3, rows - 3):
        merge(y)
    wait(copies)


def curl_ahead(v, above):
    inside = lax.broadcasted_iota(jnp.int32, v[0].shape, 0) < 7
    size = v[0].shape[1]

    def dz(c):
        return pltpu.roll(v[c], size - 1, 1) - v[c]

    def dx(c):
        return jnp.where(inside, pltpu.roll(v[c], 7, 0), 0.0) - v[c]

    return [
        (above[2] - v[2]) - dz(1),
        dz(0) - dx(2),
        dx(1) - (above[0] - v[0]),
    ]


def curl_back(v, below):
    inside = lax.broadcasted_iota(jnp.int32, v[0].shape, 0) > 0

    def dz(c):
        return v[c] - pltpu.roll(v[c], 1, 1)

    def dx(c):
        return v[c] - jnp.where(inside, pltpu.roll(v[c], 1, 0), 0.0)

    return [
        (v[2] - below[2]) - dz(1),
        dz(0) - dx(2),
        dx(1) - (v[0] - below[0]),
    ]


SCRATCH = dict(
    M=3, W=3, E1=3, Q1=3, F1=3, Q2=3, aE=3, aC=3, bH=3, cC=3, cE=3, hg=3, inv=1, g2=1, k0=1, k1=1
)


def six_stages(
    get, put, tally, held, bases, count, table, push_first, push_second, keep_row, keep_lane, flushes, arrivals
):
    def load(name, row):
        return [held[name][c, row] for c in range(SCRATCH[name])]

    def pair(name, row):
        return {0: held[name][0, row], 2: held[name][2, row]}

    def store(name, row, values):
        for c, value in enumerate(values):
            held[name][c, row] = value

    def kept(values, row):
        done = []
        for value in values:
            value = jnp.concatenate([value[:, :256], value[:, 256:] * keep_lane], 1)
            done.append(value if keep_row is None else value * keep_row(row))
        return done

    def trio(name, row):
        return [get((name, c), row) for c in range(3)]

    def stage_one(r):
        above = {0: get(("E", 0), r + 1), 2: get(("E", 2), r + 1)}
        curl = curl_ahead(trio("E", r), above)
        store("M", r, kept([h - 0.5 * c for h, c in zip(trio("H", r), curl)], r))

    def stage_two(r):
        electric, polar, rate = trio("E", r), trio("P", r), trio("Q", r)
        upper, lower = get(("N", 0), r), get(("N", 1), r)
        label, gain, source = get(("lab", 0), r), get(("gain", 0), r), get(("src", 0), r)
        inverse = jnp.zeros_like(label)
        for m, value in enumerate(table):
            inverse = jnp.where(label == m + 1.0, value, inverse)
        g2, g4 = 0.2 * gain, 0.4 * gain
        k0 = g4 * (upper - lower)
        q1 = [0.9 * q - 0.3 * p + k0 * e for q, p, e in zip(rate, polar, electric)]
        p1 = [p + 0.5 * q for p, q in zip(polar, q1)]
        curl = curl_back(load("M", r), pair("M", r - 1))
        f1 = [0.5 * (c - q) for c, q in zip(curl, q1)]
        f1[2] = f1[2] - push_first * source
        e1 = [e + inverse * f for e, f in zip(electric, f1)]
        s1 = g2 * sum(e * q for e, q in zip(e1, q1))
        up = upper + 0.5 * (0.05 * (1.0 - upper - lower) - 0.02 * upper)
        low = lower + 0.5 * (0.02 * upper - 0.3 * lower)
        k1 = g4 * (up - low - 2.0 * s1)
        q2 = [0.9 * q - 0.3 * p + k1 * e for q, p, e in zip(q1, p1, e1)]
        sb = g2 * (get(("Ns", 1), r) - get(("Ns", 0), r))
        a_e = [e + sb * q for e, q in zip(trio("Es", r), q2)]
        half = 0.5 * inverse
        store("E1", r, e1)
        store("Q1", r, q1)
        store("F1", r, f1)
        store("Q2", r, q2)
        store("aE", r, a_e)
        store("aC", r, [half * a for a in a_e])
        store("inv", r, [inverse])
        store("g2", r, [g2])
        store("k0", r, [k0])
        store("k1", r, [k1])

    def stage_three(r):
        curl = curl_ahead(load("E1", r), pair("E1", r + 1))
        store("W", r, kept([m - 0.5 * c for m, c in zip(load("M", r), curl)], r))
        curl = curl_ahead(load("aC", r), pair("aC", r + 1))
        store("bH", r, kept([h + c for h, c in zip(trio("Hs", r), curl)], r))

    def stage_four(r):
        (inverse,), (g2,), (k0,), (k1,) = load("inv", r), load("g2", r), load("k0", r), load("k1", r)
        up, low = get(("Ns", 0), r), get(("Ns", 1), r)
        sb = g2 * (low - up)
        curl = curl_back(load("W", r), pair("W", r - 1))
        q2, e1, a_e = load("Q2", r), load("E1", r), load("aE", r)
        f2 = [0.5 * (c - q) for c, q in zip(curl, q2)]
        f2[2] = f2[2] - push_second * get(("src", 0), r)
        e2 = [e + inverse * f for e, f in zip(e1, f2)]
        grad = sum(a[:, :256] * f[:, :256] for a, f in zip(a_e, f2))
        p_seed = trio("Ps", r)
        qt = [
            q + sb * e + 0.5 * (p - inverse * a)
            for q, e, p, a in zip(trio("Qs", r), e2, p_seed, a_e)
        ]
        dn = 2.0 * g2 * sum(q * e for q, e in zip(qt, e1))
        a_up = 0.965 * up + 0.01 * low + dn
        a_low = 0.85 * low - 0.025 * up - dn
        curl = curl_back(load("bH", r), pair("bH", r - 1))
        sb = g2 * (a_low - a_up)
        c_e = [
            a + k1 * q - 0.5 * c + sb * p for a, q, c, p in zip(a_e, qt, curl, load("Q1", r))
        ]
        half = 0.5 * inverse
        store("cC", r, [half * c for c in c_e])

        def own(value):
            return value[:, :256]

        grad = grad + sum(own(c) * own(f) for c, f in zip(c_e, load("F1", r)))
        inverse, g2, k0, sb = own(inverse), own(g2), own(k0), own(sb)
        p_out, q_out = [], []
        dn = 0.0
        for c in range(3):
            a_p = own(p_seed[c]) - 0.3 * own(qt[c])
            pt = a_p - inverse * own(c_e[c])
            q = 0.9 * own(qt[c]) + sb * own(e1[c]) + 0.5 * pt
            p_out.append(a_p - 0.3 * q)
            q_out.append(0.9 * q)
            dn = dn + q * own(get(("E", c), r))
            held["cE"][c, r] = own(c_e[c]) + k0 * q
        dn = 2.0 * g2 * dn
        a_up, a_low = own(a_up), own(a_low)
        put("polar", r, p_out)
        put("rate", r, q_out)
        put("levels", r, [0.965 * a_up + 0.01 * a_low + dn, 0.85 * a_low - 0.025 * a_up - dn])
        put("cell", r, [grad])

    def stage_five(r):
        curl = curl_ahead(load("cC", r), pair("cC", r + 1))
        store("hg", r, kept([h + c for h, c in zip(load("bH", r), curl)], r))

    def stage_six(r):
        hg = load("hg", r)
        curl = curl_back(hg, pair("hg", r - 1))
        put("h", r, [h[:, :256] for h in hg])
        put("e", r, [held["cE"][c, r] - 0.5 * curl[c][:, :256] for c in range(3)])
        tally(r)

    plan = (
        (stage_six, 7, 3, count - 3),
        (stage_five, 6, 2, count - 3),
        (stage_four, 4, 2, count - 2),
        (stage_three, 3, 1, count - 2),
        (stage_two, 1, 1, count - 1),
        (stage_one, 0, 0, count - 1),
    )
    marks = {low + lag for _, lag, low, high in plan} | {high + lag for _, lag, low, high in plan}
    marks = sorted(marks | {row + 7 for row in flushes})
    for begin, end in zip(marks, marks[1:]):
        active = [(f, lag) for f, lag, low, high in plan if low + lag <= begin and end <= high + lag]

        def body(i, carry, active=active):
            for f, lag in active:
                for base in bases:
                    f(i - lag + base)
            return carry

        if begin in arrivals:
            arrivals[begin]()
        if end - begin == 1:
            body(begin, 0)
        else:
            lax.fori_loop(begin, end, body, 0)
        if end - 7 in flushes:
            flushes[end - 7]()


OUTS = ("e", "h", "polar", "rate", "levels", "cell")
OUT_COMPS = dict(e=3, h=3, polar=3, rate=3, levels=2, cell=1)
HELD = tuple(SCRATCH)


def lane_keep():
    lane = lane_of((1, 128))
    outside = jnp.logical_and(lax.axis_index("gz") == 0, lane >= 64)
    return jnp.where(outside, 0.0, 1.0).astype(F32)


def material_sums(totals, label, value):
    for m in range(totals.shape[0]):
        totals[m] = totals[m] + jnp.where(label == m + 1.0, value, 0.0)


def leave(staged, outs, base, target, count, sems):
    copies = []
    for i, name in enumerate(OUTS):
        if OUT_COMPS[name] == 1:
            source = staged[name].at[0, pl.ds(base, count)]
            goal = outs[name].at[pl.ds(target, count)]
        else:
            source = staged[name].at[:, pl.ds(base, count)]
            goal = outs[name].at[:, pl.ds(target, count)]
        copies.append(pltpu.make_async_copy(source, goal, sems.at[i]))
    return go(copies)


def inner_kernel(rows, *refs):
    n = len(NAMES)
    sources = refs[: n + 1]
    table_ref, push_ref = refs[n + 1 : n + 3]
    at = n + 3
    outs = dict(zip(OUTS, refs[at : at + len(OUTS)]))
    totals, ext = refs[at + len(OUTS) : at + len(OUTS) + 2]
    at += len(OUTS) + 2
    inputs = refs[at : at + n + 1]
    given, tiles = dict(zip(NAMES, inputs[:n])), inputs[n]
    at += n + 1
    staged = dict(zip(OUTS, refs[at : at + len(OUTS)]))
    at += len(OUTS)
    held = dict(zip(HELD, refs[at : at + len(HELD)]))
    load_sems, sems = refs[at + len(HELD) :]

    arrivals = {}
    begins = {0: 0, 6: 7, 10: 11, 21: 22}
    bounds = list(begins.values()) + [rows]
    for piece, mark in enumerate(begins):
        low, high = bounds[piece], bounds[piece + 1]
        copies = []
        for i, (source, target) in enumerate(zip(sources, inputs)):
            where = pl.ds(low, high - low)
            if len(source.shape) == 4:
                source, target = source.at[:, where], target.at[:, where]
            else:
                source, target = source.at[where], target.at[where]
            copies.append(pltpu.make_async_copy(source, target, load_sems.at[piece, i]))
        go(copies)
        arrivals[mark] = lambda copies=copies: wait(copies)
    totals[...] = jnp.zeros_like(totals)

    def get(comp, r):
        third = pltpu.roll(tiles[r], 128 - SPOT[comp], 1)
        return jnp.concatenate([pull(given[comp[0]], comp, r), third], 1)

    def put(name, r, values):
        for c, value in enumerate(values):
            staged[name][c, r] = value

    def tally(r):
        material_sums(totals, given["lab"][r].astype(F32) + 1.0, staged["cell"][0, r])

    copies = []
    cuts = [3, 14, 22, rows - 3]

    def flush(piece):
        low, high = cuts[piece], cuts[piece + 1]
        copies.extend(leave(staged, outs, low, low, high - low, sems.at[piece]))

    flushes = {cuts[piece + 1]: (lambda piece=piece: flush(piece)) for piece in range(3)}
    six_stages(
        get,
        put,
        tally,
        held,
        (0,),
        rows,
        [table_ref[m] for m in range(table_ref.shape[0])],
        push_ref[0],
        push_ref[1],
        None,
        lane_keep(),
        flushes,
        arrivals,
    )

    def hand_on(k, carry):
        for comp in COMPS:
            ext[INDEX[comp], k] = get(comp, k)
            ext[INDEX[comp], 6 + k] = get(comp, rows - 6 + k)
        return carry

    lax.fori_loop(0, 6, hand_on, 0)
    wait(copies)


def edge_kernel(rows, scale, near, far, own, inner_totals, table_ref, push_ref, *refs):
    outs = dict(zip(OUTS, refs[len(OUTS) : 2 * len(OUTS)]))
    sent, ext, totals = refs[2 * len(OUTS) : 2 * len(OUTS) + 3]
    at = 2 * len(OUTS) + 3
    staged = dict(zip(OUTS, refs[at : at + len(OUTS)]))
    at += len(OUTS)
    held = dict(zip(HELD, refs[at : at + len(HELD)]))
    sems = refs[at + len(HELD)]
    even = lax.rem(lax.axis_index("gy"), 2) == 0
    top = lax.axis_index("gy") == 0
    totals[...] = inner_totals[...]

    def arrived(side, plane):
        use_far = even if side == 0 else jnp.logical_not(even)
        return jnp.where(use_far, far[plane].astype(F32), near[plane].astype(F32))

    for side in range(2):
        tiles = []
        for t in range(3):
            tile = arrived(side, CORNERS + t // 2)
            tiles.append(tile[:, (t % 2) * 128 : (t % 2) * 128 + 128])
        for comp in COMPS:
            w = WIDTH[comp[0]]
            for k in range(w):
                r = 3 - w + k if side == 0 else 6 + k
                main = arrived(side, PLANE[comp] + k)
                if comp[0] == "Hs" and r == (2 if side == 0 else 6):
                    main = main + arrived(side, LOW_BITS + comp[1])
                third = pltpu.roll(tiles[r if side == 0 else r - 6], 128 - SPOT[comp], 1)
                ext[INDEX[comp], side * EDGE + r] = jnp.concatenate([main, third], 1)

    def bring(k, carry):
        for comp in COMPS:
            ext[INDEX[comp], 3 + k] = own[INDEX[comp], k]
        return carry

    lax.fori_loop(0, 12, bring, 0)

    def get(comp, r):
        return ext[INDEX[comp], r]

    def put(name, r, values):
        for c, value in enumerate(values):
            staged[name][c, r] = value

    def keep_row(r):
        return jnp.where(jnp.logical_and(top, r < 3), 0.0, 1.0).astype(F32)

    def tally(r):
        material_sums(totals, ext[INDEX[("lab", 0)], r, :, :256], staged["cell"][0, r])

    six_stages(
        get,
        put,
        tally,
        held,
        (0, EDGE),
        EDGE,
        [table_ref[m] for m in range(table_ref.shape[0])],
        push_ref[0],
        push_ref[1],
        keep_row,
        lane_keep(),
        {},
        {},
    )
    copies = []
    for side in range(2):
        start = 0 if side == 0 else rows - 3
        copies += leave(staged, outs, side * EDGE + 3, start, 3, sems.at[side])
    lane = lane_of((1, 128))
    line = jnp.zeros((1, 128), F32)
    for m in range(totals.shape[0]):
        line = jnp.where(lane == m, jnp.sum(totals[m]) * scale, line)
    sent[...] = jnp.broadcast_to(line[None], sent.shape)
    wait(copies)


def swapped(block, axes, odd):
    size = [lax.axis_size(a) for a in ("gy", "gz")]
    pairs = []
    for y in range(size[0]):
        for z in range(size[1]):
            y2, z2 = (y + 1, z) if axes == "gy" else (y, z + 1)
            at = y if axes == "gy" else z
            if at % 2 == odd and y2 < size[0] and z2 < size[1]:
                one, two = y * size[1] + z, y2 * size[1] + z2
                pairs += [(one, two), (two, one)]
    return lax.ppermute(block, ("gy", "gz"), pairs)


def on_device(
    efield_check,
    hfield_check,
    polar_check,
    rate_check,
    levels_check,
    efield_seed,
    hfield_seed,
    polar_seed,
    rate_seed,
    levels_seed,
    material_labels,
    gain_labels,
    inverse_table,
    source_field,
    start_step,
):
    given = (
        efield_check,
        hfield_check,
        polar_check,
        rate_check,
        levels_check,
        material_labels,
        gain_labels,
        source_field,
        efield_seed,
        levels_seed,
        hfield_seed,
        polar_seed,
        rate_seed,
    )
    fixed = [pltpu.with_memory_space_constraint(array, pltpu.HBM) for array in given]
    rows = material_labels.shape[0]
    count = inverse_table.shape[0]
    start = start_step[0].astype(F32)
    pushes = jnp.stack([jnp.sin(SOURCE_OMEGA * start), jnp.sin(SOURCE_OMEGA * (start + 1.0))])
    hbm = pl.BlockSpec(memory_space=pltpu.HBM)
    anywhere = pl.BlockSpec(memory_space=pl.ANY)
    vmem = pl.BlockSpec(memory_space=pltpu.VMEM)
    smem = pl.BlockSpec(memory_space=pltpu.SMEM)
    tile_shape = jax.ShapeDtypeStruct((rows, 8, 128), BF16)
    message = jax.ShapeDtypeStruct((PLANES, 8, 256), BF16)
    blocks = 4

    def row_block(array):
        if array.ndim == 3:
            return pl.BlockSpec((rows // blocks, 8, 256), lambda i: (i, 0, 0))
        return pl.BlockSpec((array.shape[0], rows // blocks, 8, 256), lambda i: (0, i, 0, 0))

    def grant(mib):
        return pltpu.CompilerParams(vmem_limit_bytes=mib * 1024 * 1024)

    tile_block = pl.BlockSpec((rows // blocks, 8, 128), lambda i: (i, 0, 0))
    send_edges, send_near, send_far = pl.pallas_call(
        lambda *refs: pack_kernel(rows, *refs),
        grid=(blocks,),
        out_shape=(tile_shape, message, message),
        in_specs=[row_block(array) for array in given] + [hbm] * len(given),
        out_specs=(tile_block, hbm, hbm),
        scratch_shapes=[
            pltpu.VMEM((2, PLANES, 8, 256), BF16),
            pltpu.VMEM((2, 24, 8, 256), F32),
            pltpu.VMEM((2, 4, 8, 256), jnp.int32),
            pltpu.SemaphoreType.DMA((2, len(COMPS))),
            pltpu.SemaphoreType.DMA((2,)),
        ],
        compiler_params=grant(60),
        name="pack_kernel",
    )(*given, *given)
    first = swapped(send_edges, "gz", 0)
    second = swapped(send_edges, "gz", 1)
    tiles, send_near, send_far = pl.pallas_call(
        lambda *refs: corner_kernel(rows, *refs),
        out_shape=(jax.ShapeDtypeStruct((rows, 8, 128), F32), message, message),
        in_specs=[vmem, vmem, smem, hbm, hbm],
        out_specs=(vmem, hbm, hbm),
        scratch_shapes=[
            pltpu.VMEM((2, 2, 8, 256), BF16),
            pltpu.SemaphoreType.DMA((2,)),
        ],
        input_output_aliases={3: 1, 4: 2},
        compiler_params=grant(4),
        name="corner_kernel",
    )(first, second, pushes, send_near, send_far)
    far = swapped(send_far, "gy", 1)
    near = swapped(send_near, "gy", 0)

    def out_shape(name):
        dims = (rows, 8, 256)
        return jax.ShapeDtypeStruct(dims if OUT_COMPS[name] == 1 else (OUT_COMPS[name],) + dims, F32)

    def local(size):
        return [
            pltpu.VMEM((SCRATCH[name], size, 8, 256 if name == "cE" else LANES), F32)
            for name in HELD
        ]

    def copy_of(array, size):
        return pltpu.VMEM(array.shape[:-3] + (size,) + array.shape[-2:], array.dtype)

    sums = jax.ShapeDtypeStruct((count, 8, 256), F32)
    handed = jax.ShapeDtypeStruct((len(COMPS), 12, 8, LANES), F32)
    *inner, totals, own = pl.pallas_call(
        lambda *refs: inner_kernel(rows, *refs),
        out_shape=tuple(out_shape(name) for name in OUTS) + (sums, handed),
        in_specs=[hbm] * len(given) + [anywhere, smem, smem],
        out_specs=(hbm,) * len(OUTS) + (vmem, vmem),
        scratch_shapes=[copy_of(array, rows) for array in (*given, tiles)]
        + [pltpu.VMEM((OUT_COMPS[name], rows, 8, 256), F32) for name in OUTS]
        + local(rows)
        + [
            pltpu.SemaphoreType.DMA((4, len(given) + 1)),
            pltpu.SemaphoreType.DMA((3, len(OUTS))),
        ],
        compiler_params=grant(32),
        cost_estimate=pl.CostEstimate(flops=40_000_000, bytes_accessed=12_000_000, transcendentals=0),
        name="inner_rows",
    )(*fixed, tiles, inverse_table, pushes)

    devices = lax.axis_size("gy") * lax.axis_size("gz")
    cells = rows * material_labels.shape[1] * material_labels.shape[2] * devices
    *outs, sent = pl.pallas_call(
        lambda *refs: edge_kernel(rows, 1.0 / math.sqrt(cells), *refs),
        out_shape=tuple(out_shape(name) for name in OUTS)
        + (jax.ShapeDtypeStruct((devices, 1, 128), F32),),
        in_specs=[vmem] * 4 + [smem, smem] + [hbm] * len(OUTS),
        out_specs=(hbm,) * len(OUTS) + (vmem,),
        scratch_shapes=[
            pltpu.VMEM((len(COMPS), 2 * EDGE, 8, LANES), F32),
            pltpu.VMEM((count, 8, 256), F32),
        ]
        + [pltpu.VMEM((OUT_COMPS[name], 2 * EDGE, 8, 256), F32) for name in OUTS]
        + local(2 * EDGE)
        + [pltpu.SemaphoreType.DMA((2, len(OUTS)))],
        input_output_aliases={6 + i: i for i in range(len(OUTS))},
        compiler_params=grant(26),
        cost_estimate=pl.CostEstimate(flops=16_000_000, bytes_accessed=6_000_000, transcendentals=0),
        name="edge_rows",
    )(near, far, own, totals, inverse_table, pushes, *inner)
    parts = lax.all_to_all(sent, ("gy", "gz"), 0, 0)
    table_grad = jnp.sum(parts[:, 0, :count], axis=0)
    return (*outs, table_grad)


def solution(mesh):
    field = P(None, "gy", None, "gz")
    cell = P("gy", None, "gz")
    return jax.shard_map(
        on_device,
        mesh=mesh,
        in_specs=(field,) * 10 + (cell, cell, P(), cell, P()),
        out_specs=(field,) * 5 + (cell, P()),
        check_vma=False,
    )
```
